32 devices in a mesh: field: 2 (over y), epoch: 4 (over z), sky: 4 (over x, core).
Axes of the slice: x: 2, y: 2, z: 4, core: 2. Of those that a mesh axis runs over, the one named last changes fastest.
Arguments:
- sky_scene: bfloat16 [4096, 2048], P(('field', 'epoch'), 'sky'), parts along dimension 0, may hold values from -6 to 6
- images: bfloat16 [16, 2048, 2048], P(('field', 'epoch'), None, 'sky'), parts along dimension 0, may hold values from -6 to 6
- psf_rows: bfloat16 [16, 25], P('field'), parts along dimension 0, may hold values from 0.0099487305 to 0.06982422
- psf_cols: bfloat16 [16, 25], P('field'), parts along dimension 0, may hold values from 0.0099487305 to 0.06982422
- offsets: int32 [16, 2], P('field'), parts along dimension 0, may hold values from -4 to 4, as said below
- epoch_weight: float32 [16], P('field'), parts along dimension 0, may hold values from 0.25 to 2
- column_mask: int32 [16, 2048], P('field', 'sky'), parts along dimension 0, may hold values 0 or 1
- coverage: int32 [16, 4, 4], P('field'), parts along dimension 0, may hold values from 0 to 1, as said below
Outputs:
- gradient: float32 [4096, 2048], P(('field', 'epoch'), 'sky'), parts along dimension 0
The draws below stay inside these ranges and needn't reach their ends.
There are 2 independent parts, one for each index of `field`. The reference program is written for one: setup_inputs(seed, part) draws one part's arguments, and reference() takes and returns one part's arrays. A program takes and returns all parts, laid end to end along the dimension named above; each array names one. Nothing has to cross between parts.
Inputs may be any that keep to these rules, and one draw needn't show every extreme that they name: `offsets`: column 0 shifts rows and column 1 shifts columns. `coverage`: the tiles that one epoch covers form a rectangle of whole tiles that spans all tile rows or all but one of them, and all tile columns or all but one of them.
All inputs are finite; a program needn't handle non-finite values. No bound on the sum of `column_mask` on one device may be relied on, other than what follows from the above.
Results may differ from the reference program's by a relative error of at most 0.0045.
Values may be sent and summed in bfloat16 or wider, within the bound.
A program may use at most 64 MiB of HBM per device.

```python
import math
import jax
import jax.numpy as jnp
from jax import lax

H = 2048
W = 2048
TILE = 512
KW = 25
MAXOFF = 4
PR = 12
HALO = 16
EPOCHS = 8
TROWS = 4
TCOLS = 4


def draw_offsets(key, part):
    values = jax.random.randint(key, (EPOCHS, 2), -MAXOFF, MAXOFF + 1)
    values = values.at[0, 0].set(MAXOFF).at[0, 1].set(-MAXOFF)
    values = values.at[1, 0].set(-MAXOFF).at[1, 1].set(MAXOFF)
    return values.astype(jnp.int32)


def footprint(key_length, key_start, count):
    shortest = max(count - 1, 1)
    span = jax.random.randint(key_length, (EPOCHS,), shortest, count + 1)
    first = jax.random.randint(key_start, (EPOCHS,), 0, count - span + 1)
    index = jnp.arange(count)[None, :]
    return (index >= first[:, None]) & (index < (first + span)[:, None])


def draw_coverage(key, part):
    key_rowa, key_rowb, key_cola, key_colb = jax.random.split(key, 4)
    inside_rows = footprint(key_rowa, key_rowb, TROWS)
    inside_cols = footprint(key_cola, key_colb, TCOLS)
    return (inside_rows[:, :, None] & inside_cols[:, None, :]).astype(jnp.int32)


def with_ends(values, key, smallest, high):
    longest = values.shape.index(max(values.shape))
    spots = []
    for shift in (0, 1):
        where = [jax.random.randint(jax.random.fold_in(key, axis), (), 0, length) for axis, length in enumerate(values.shape)]
        where[longest] = (where[longest] + shift) % values.shape[longest]
        spots.append(tuple(where))
    return values.at[spots[0]].set(smallest).at[spots[1]].set(high)


def steps_of(rng, extent, pieces, low, largest):
    factor_of = 1.0
    for position, shards_of in pieces:
        steps = jax.random.uniform(jax.random.fold_in(jax.random.fold_in(rng, 6), position), (shards_of,), jnp.float32, low / len(pieces), largest / len(pieces))
        factor_of = factor_of * jnp.repeat(jnp.exp(steps), extent[position] // shards_of).reshape((-1,) + (1,) * (len(extent) - 1 - position))
    return factor_of


def gaussian(stream_key, shape, width, bound, cuts=(), dtype=jnp.bfloat16):
    values = width * jax.random.normal(stream_key, shape, jnp.float32)
    if cuts:
        values = values * steps_of(stream_key, shape, cuts, -0.22, 0.18)
    return jnp.clip(values, -bound, bound).astype(dtype)


def setup_inputs(seed: int = 0, part: int = 0) -> dict:
    key_of = jax.random.split(jax.random.key(seed), 9)
    part_keys = jax.random.split(jax.random.fold_in(key_of[8], part), 9)
    sky_scene = gaussian(part_keys[0], (H, W), 1.0, 6.0, ((0, 4), (1, 4)))
    images = gaussian(part_keys[1], (EPOCHS, H, W), 1.0, 6.0, ((0, 4), (2, 4)))
    psf_rows = jnp.clip(jax.random.uniform(part_keys[2], (EPOCHS, KW), jnp.float32, 0.0099487305, 0.06982422), 0.0099487305, 0.06982422).astype(jnp.bfloat16)
    psf_cols = jnp.clip(jax.random.uniform(part_keys[3], (EPOCHS, KW), jnp.float32, 0.0099487305, 0.06982422), 0.0099487305, 0.06982422).astype(jnp.bfloat16)
    offsets = draw_offsets(jax.random.fold_in(jax.random.fold_in(key_of[8], part), 71), part)
    epoch_weight = jnp.clip(jnp.exp(jax.random.uniform(part_keys[5], (EPOCHS,), jnp.float32, math.log(0.25), math.log(2.0))), 0.25, 2.0)
    column_mask = with_ends((jax.random.randint(part_keys[6], (EPOCHS, W), 0, 16) < 15).astype(jnp.int32), jax.random.fold_in(part_keys[6], 1), 0, 1)
    coverage = draw_coverage(jax.random.fold_in(jax.random.fold_in(key_of[8], part), 71), part)
    return dict(sky_scene=sky_scene, images=images, psf_rows=psf_rows, psf_cols=psf_cols, offsets=offsets, epoch_weight=epoch_weight, column_mask=column_mask, coverage=coverage)


def correlate(plane_in, kernel, shift_by, along):
    length_out = plane_in.shape[along]
    if along == 0:
        padded = jnp.pad(plane_in, ((HALO, HALO), (0, 0)))
        weights = kernel.reshape(1, 1, KW, 1)
    else:
        padded = jnp.pad(plane_in, ((0, 0), (HALO, HALO)))
        weights = kernel.reshape(1, 1, 1, KW)
    begin = (HALO - PR + shift_by).astype(jnp.int32)
    window = lax.dynamic_slice_in_dim(padded, begin, length_out + KW - 1, along)
    result = lax.conv_general_dilated(window[None, None], weights, (1, 1), "VALID", precision=lax.Precision.HIGHEST)
    return result[0, 0]


def rounded(values):
    narrow = values.astype(jnp.bfloat16)
    narrow = lax.optimization_barrier(narrow)
    return narrow.astype(jnp.float32)


def reference(sky_scene, images, psf_rows, psf_cols, offsets, epoch_weight, column_mask, coverage):
    rows_tile = jnp.arange(H) // TILE
    cols_tile = jnp.arange(W) // TILE
    scene_wide = sky_scene.astype(jnp.float32)

    def one_epoch(running, item):
        observed, kernel_row, kernel_col, band_shift, weight, mask_row, tile_cover = item
        kernel_row = kernel_row.astype(jnp.float32)
        kernel_col = kernel_col.astype(jnp.float32)
        lifted = rounded(correlate(scene_wide, kernel_row, band_shift[0], 0))
        modeled = correlate(lifted, kernel_col, band_shift[1], 1)
        tile_map = tile_cover[rows_tile][:, cols_tile].astype(jnp.float32)
        factor = (2.0 * weight * tile_map) * mask_row.astype(jnp.float32)[None, :]
        residual = rounded(factor * (modeled - observed.astype(jnp.float32)))
        pulled = rounded(correlate(residual, kernel_col[::-1], -band_shift[1], 1))
        grad_term = correlate(pulled, kernel_row[::-1], -band_shift[0], 0)
        return running + grad_term, None

    start = jnp.zeros((H, W), jnp.float32)
    running, unused = lax.scan(one_epoch, start, (images, psf_rows, psf_cols, offsets, epoch_weight, column_mask, coverage))
    return running
```

```python
import functools
import jax
import jax.numpy as jnp
from jax import lax
from jax.experimental import pallas as pl
from jax.experimental.pallas import tpu as pltpu
from jax.sharding import PartitionSpec as P

TILE = 512
HALO = 16
MESH = pl.DeviceIdType.MESH
ROWS = 512
COLS = 512
PAD = 128
WIDE = COLS + 2 * PAD
SUB = 128
REACH = SUB + 2 * HALO
CHUNK = 256
PARTS = ROWS // CHUNK


def extended(value, sides, width):
    for axis, dim in sides:
        peers, length = (lax.axis_size(axis), value.shape[dim])
        up = [(i, (i + 1) % peers) for i in range(peers - 1)]
        down = [(j, i) for i, j in up]
        last = lax.slice_in_dim(value, length - width, length, axis=dim)
        initial = lax.slice_in_dim(value, 0, width, axis=dim)
        before = lax.ppermute(last, axis, up)
        after = lax.ppermute(initial, axis, down)
        value = jnp.concatenate([before, value, after], axis=dim)
    return value


def band_tables(kernels, shifts, count_in, count_out):
    row_index = lax.broadcasted_iota(jnp.int32, (count_in, count_out), 0)
    col_index = lax.broadcasted_iota(jnp.int32, (count_in, count_out), 1)
    spread = kernels.shape[1]
    half_width = (spread - 1) // 2
    position = (
        (row_index - col_index)[None]
        - shifts[:, None, None]
        + half_width
        - (count_in - count_out) // 2
    )
    band_table = jnp.zeros((kernels.shape[0], count_in, count_out), jnp.float32)
    for each_tap in range(spread):
        band_table = band_table + jnp.where(
            position == each_tap, kernels[:, each_tap, None, None].astype(jnp.float32), 0.0
        )
    return band_table.astype(jnp.bfloat16)


def epoch_block(window, row_table, col_table, image_block, factor):
    lifted = jnp.einsum("ki,kc->ic", row_table, window, preferred_element_type=jnp.float32).astype(
        jnp.bfloat16
    )
    modeled = jnp.dot(lifted, col_table, preferred_element_type=jnp.float32)
    residual = (factor * (modeled - image_block.astype(jnp.float32))).astype(jnp.bfloat16)
    pulled = jnp.einsum(
        "ic,kc->ik", residual, col_table, preferred_element_type=jnp.float32
    ).astype(jnp.bfloat16)
    return jnp.dot(row_table, pulled, preferred_element_type=jnp.float32)


def strip_plan(sky_scene, images, psf_rows, psf_cols, offsets, epoch_weight, column_mask, coverage):
    slab_cells = extended(sky_scene, (("sky", 1),), HALO)
    strip_cells = lax.all_gather(slab_cells, "epoch", axis=0, tiled=True)
    strip_cells = jnp.pad(strip_cells, ((HALO, HALO), (0, 0)))
    full_rows = strip_cells.shape[0] - 2 * HALO
    strip_width = sky_scene.shape[1]
    local_count = images.shape[0]
    epoch_base = lax.axis_index("epoch") * local_count
    tile_column = lax.axis_index("sky") * strip_width // TILE

    def per_epoch(local_epoch, running):
        epoch_now = epoch_base + local_epoch
        row_table = band_tables(
            psf_rows[epoch_now][None], offsets[epoch_now, 0][None], TILE + 2 * HALO, TILE
        )[0]
        col_table = band_tables(
            psf_cols[epoch_now][None],
            offsets[epoch_now, 1][None],
            strip_width + 2 * HALO,
            strip_width,
        )[0]
        observed = lax.dynamic_index_in_dim(images, local_epoch, 0, keepdims=False)
        weight = epoch_weight[epoch_now]
        mask_row = column_mask[epoch_now].astype(jnp.float32)
        for row_block in range(full_rows // TILE):
            covered_flag = coverage[epoch_now, row_block, tile_column]
            window = strip_cells[row_block * TILE : row_block * TILE + TILE + 2 * HALO]
            image_block = observed[row_block * TILE : (row_block + 1) * TILE]
            factor = 2.0 * weight * covered_flag.astype(jnp.float32) * mask_row

            def covered():
                return epoch_block(window, row_table, col_table, image_block, factor)

            def skipped():
                return jnp.zeros((TILE + 2 * HALO, strip_width + 2 * HALO), jnp.float32)

            grad_term = lax.cond(covered_flag > 0, covered, skipped)
            running = running.at[row_block * TILE : row_block * TILE + TILE + 2 * HALO].add(
                grad_term
            )
        return running

    running = lax.fori_loop(
        0,
        local_count,
        per_epoch,
        jnp.zeros((full_rows + 2 * HALO, strip_width + 2 * HALO), jnp.float32),
    )
    trimmed = running[HALO : HALO + full_rows]
    packed = jnp.concatenate([trimmed[:, :HALO], trimmed[:, strip_width + HALO :]], axis=1)
    center_raw = trimmed[:, HALO : HALO + strip_width]
    received = extended(packed, (("sky", 1),), HALO)
    center_cells = center_raw.at[:, :HALO].add(received[:, :HALO])
    center_cells = center_cells.at[:, strip_width - HALO :].add(received[:, 3 * HALO :])
    return lax.psum_scatter(center_cells, "epoch", scatter_dimension=0, tiled=True)


def band(position, psf_ref, epoch, first, taps):
    table = jnp.zeros(position.shape, jnp.float32)
    for tap in range(taps):
        table = jnp.where(position == tap, psf_ref[epoch, first + tap], table)
    return table.astype(jnp.bfloat16)


def fused_kernel(
    n, sky_count, taps, local,
    psf_ref, offset_ref, factor_ref, mask_ref, scene_ref, image_ref, out_ref,
    strip, acc, image_buf, row_tab, rowt_tab, col_tab, lift, res, pull,
    edge_out, edge_in, send_r, recv_r, send_l, recv_l,
    load_sem, image_sem,
    ag_r_send, ag_r_recv, ag_l_send, ag_l_recv,
    sky_r_send, sky_r_recv, sky_l_send, sky_l_recv,
    rs_r_send, rs_r_recv, rs_l_send, rs_l_recv,
    ed_r_send, ed_r_recv, ed_l_send, ed_l_recv,
):
    me = lax.axis_index("epoch")
    sky = lax.axis_index("sky")
    total = n * ROWS
    has_up, has_down = me > 0, me < n - 1
    has_left, has_right = sky > 0, sky < sky_count - 1
    base = me * local
    half = (taps - 1) // 2

    def rows_of(block, part=None):
        if part is None:
            return pl.ds(pl.multiple_of(HALO + block * ROWS, HALO), ROWS)
        return pl.ds(pl.multiple_of(HALO + block * ROWS + part * CHUNK, HALO), CHUNK)

    centre = pl.ds(PAD, COLS)
    load = pltpu.make_async_copy(scene_ref, strip.at[rows_of(me), centre], load_sem)
    load.start()
    image_loads = [
        pltpu.make_async_copy(image_ref.at[e], image_buf.at[e], image_sem.at[e])
        for e in range(local)
    ]

    barrier = pltpu.get_barrier_semaphore()
    greetings = (
        (has_up, {"epoch": me - 1}),
        (has_down, {"epoch": me + 1}),
        (has_left, {"sky": sky - 1}),
        (has_right, {"sky": sky + 1}),
    )
    for there, where in greetings:
        @pl.when(there)
        def _():
            pl.semaphore_signal(barrier, inc=1, device_id=where, device_id_type=MESH)
    pl.semaphore_wait(barrier, sum(there.astype(jnp.int32) for there, where in greetings))

    def remote(src, dst, ssem, rsem, where):
        return pltpu.make_async_remote_copy(
            src_ref=src, dst_ref=dst, send_sem=ssem, recv_sem=rsem,
            device_id=where, device_id_type=MESH,
        )

    def gather_down(t, part):
        piece = strip.at[rows_of(me - t, part), centre]
        return remote(piece, piece, ag_r_send.at[t, part], ag_r_recv.at[t, part], {"epoch": me + 1})

    def gather_down_in(t, part):
        piece = strip.at[rows_of(me - 1 - t, part), centre]
        return remote(piece, piece, ag_r_send.at[t, part], ag_r_recv.at[t, part], {"epoch": me - 1})

    def gather_up(t, part):
        piece = strip.at[rows_of(me + t, part), centre]
        return remote(piece, piece, ag_l_send.at[t, part], ag_l_recv.at[t, part], {"epoch": me - 1})

    def gather_up_in(t, part):
        piece = strip.at[rows_of(me + 1 + t, part), centre]
        return remote(piece, piece, ag_l_send.at[t, part], ag_l_recv.at[t, part], {"epoch": me + 1})

    def sky_right(block):
        return remote(
            strip.at[rows_of(block), pl.ds(COLS, PAD)], strip.at[rows_of(block), pl.ds(0, PAD)],
            sky_r_send.at[block], sky_r_recv.at[block], {"sky": sky + 1},
        )

    def sky_right_in(block):
        return remote(
            strip.at[rows_of(block), pl.ds(COLS, PAD)], strip.at[rows_of(block), pl.ds(0, PAD)],
            sky_r_send.at[block], sky_r_recv.at[block], {"sky": sky - 1},
        )

    def sky_left(block):
        return remote(
            strip.at[rows_of(block), pl.ds(PAD, PAD)], strip.at[rows_of(block), pl.ds(PAD + COLS, PAD)],
            sky_l_send.at[block], sky_l_recv.at[block], {"sky": sky - 1},
        )

    def sky_left_in(block):
        return remote(
            strip.at[rows_of(block), pl.ds(PAD, PAD)], strip.at[rows_of(block), pl.ds(PAD + COLS, PAD)],
            sky_l_send.at[block], sky_l_recv.at[block], {"sky": sky + 1},
        )

    def send_edges(block):
        @pl.when(has_right)
        def _():
            sky_right(block).start()

        @pl.when(has_left)
        def _():
            sky_left(block).start()

    def wait_edges(block):
        @pl.when(has_left)
        def _():
            sky_right_in(block).wait_recv()

        @pl.when(has_right)
        def _():
            sky_left_in(block).wait_recv()

    load.wait()
    for part in range(PARTS):
        @pl.when(has_down)
        def _():
            gather_down(0, part).start()

        @pl.when(has_up)
        def _():
            gather_up(0, part).start()
    send_edges(me)
    for copy in image_loads:
        copy.start()

    strip[pl.ds(0, HALO), :] = jnp.zeros((HALO, WIDE), jnp.bfloat16)
    strip[pl.ds(HALO + total, HALO), :] = jnp.zeros((HALO, WIDE), jnp.bfloat16)

    @pl.when(sky == 0)
    def _():
        strip[pl.ds(HALO, total), pl.ds(0, PAD)] = jnp.zeros((total, PAD), jnp.bfloat16)

    @pl.when(sky == sky_count - 1)
    def _():
        strip[pl.ds(HALO, total), pl.ds(PAD + COLS, PAD)] = jnp.zeros((total, PAD), jnp.bfloat16)

    def clear(i, carry):
        acc[pl.ds(pl.multiple_of(i * 32, 32), 32), :] = jnp.zeros((32, WIDE), jnp.float32)
        return carry

    lax.fori_loop(0, (total + 2 * HALO) // 32, clear, 0)

    for e in range(local):
        shift_r = offset_ref[base + e, 0]
        shift_c = offset_ref[base + e, 1]
        out_i = lax.broadcasted_iota(jnp.int32, (SUB, REACH), 0)
        in_i = lax.broadcasted_iota(jnp.int32, (SUB, REACH), 1)
        row_tab[e] = band(in_i - out_i - HALO - shift_r + half, psf_ref, base + e, 0, taps)
        in_t = lax.broadcasted_iota(jnp.int32, (REACH, SUB), 0)
        out_t = lax.broadcasted_iota(jnp.int32, (REACH, SUB), 1)
        rowt_tab[:, e * SUB : (e + 1) * SUB] = band(
            in_t - out_t - HALO - shift_r + half, psf_ref, base + e, 0, taps
        )

        def fill(i, carry):
            k = lax.broadcasted_iota(jnp.int32, (64, 256), 0) + i * 64
            j = lax.broadcasted_iota(jnp.int32, (64, 256), 1)
            col_tab[e, pl.ds(pl.multiple_of(i * 64, 64), 64), :] = band(
                k - j - PAD - shift_c + half, psf_ref, base + e, taps, taps
            )
            return carry

        lax.fori_loop(0, 8, fill, 0)

    def compute(q, carry):
        r0 = pl.multiple_of(q * CHUNK, CHUNK)
        for e in range(local):
            for u in range(2):
                window = strip[pl.ds(pl.multiple_of(r0 + u * SUB, SUB), REACH), :]
                lift[u * SUB : (u + 1) * SUB, :] = jnp.dot(
                    row_tab[e], window, preferred_element_type=jnp.float32
                ).astype(jnp.bfloat16)
            factor = factor_ref[base + e, q // PARTS] * mask_ref[pl.ds(base + e, 1), :].astype(
                jnp.float32
            )
            for h in range(2):
                cols = slice(h * 256, (h + 1) * 256)
                modeled = jnp.dot(
                    lift[:, h * 256 : h * 256 + 512], col_tab[e], preferred_element_type=jnp.float32
                )
                seen = image_buf[e, pl.ds(r0, CHUNK), cols].astype(jnp.float32)
                res[:, cols] = (factor[:, cols] * (modeled - seen)).astype(jnp.bfloat16)

            def back(h, side):
                return lax.dot_general(
                    res[:, h * 256 : (h + 1) * 256],
                    col_tab[e, side * 256 : (side + 1) * 256, :],
                    (((1,), (1,)), ((), ())),
                    preferred_element_type=jnp.float32,
                )

            pulls = (back(0, 0), back(0, 1) + back(1, 0), back(1, 1))
            for third, value in enumerate(pulls):
                narrow = value.astype(jnp.bfloat16)
                for u in range(2):
                    pull[u, e * SUB : (e + 1) * SUB, third * 256 : (third + 1) * 256] = narrow[
                        u * SUB : (u + 1) * SUB
                    ]
        for u in range(2):
            where = pl.ds(pl.multiple_of(r0 + u * SUB, SUB), REACH)
            acc[where, :] += jnp.dot(rowt_tab[...], pull[u], preferred_element_type=jnp.float32)
        return carry

    for copy in image_loads:
        copy.wait()
    wait_edges(me)

    def ready(t):
        low = jnp.maximum(me - t, 0)
        high = jnp.minimum(me + t, n - 1)
        first = jnp.where(low == 0, 0, low + 1)
        stop = jnp.where(high == n - 1, n, high)
        return first, jnp.maximum(stop, first)

    for t in range(n - 1):
        for part in range(PARTS):
            @pl.when(me - 1 - t >= 0)
            def _():
                gather_down_in(t, part).wait_recv()
                if t + 1 < n - 1:
                    @pl.when(has_down)
                    def _():
                        gather_down(t + 1, part).start()

            @pl.when(me + 1 + t <= n - 1)
            def _():
                gather_up_in(t, part).wait_recv()
                if t + 1 < n - 1:
                    @pl.when(has_up)
                    def _():
                        gather_up(t + 1, part).start()

        @pl.when(me - 1 - t >= 0)
        def _():
            send_edges(me - 1 - t)

        @pl.when(me + 1 + t <= n - 1)
        def _():
            send_edges(me + 1 + t)

        @pl.when(me - 1 - t >= 0)
        def _():
            wait_edges(me - 1 - t)

        @pl.when(me + 1 + t <= n - 1)
        def _():
            wait_edges(me + 1 + t)

        first, stop = ready(t + 1)
        if t == 0:
            lax.fori_loop(first * PARTS, stop * PARTS, compute, 0)
        else:
            done_first, done_stop = ready(t)
            empty = done_stop <= done_first
            below_stop = jnp.where(empty, stop, done_first)
            above_first = jnp.where(empty, stop, done_stop)
            lax.fori_loop(first * PARTS, below_stop * PARTS, compute, 0)
            lax.fori_loop(above_first * PARTS, stop * PARTS, compute, 0)

    def grad_right(block, where):
        return remote(edge_out.at[1, block], edge_in.at[0, block], ed_r_send.at[block], ed_r_recv.at[block], where)

    def grad_left(block, where):
        return remote(edge_out.at[0, block], edge_in.at[1, block], ed_l_send.at[block], ed_l_recv.at[block], where)

    order = []
    for k in range(n):
        for block in (n - 1 - k, k):
            if block not in order:
                order.append(block)
    for block in order:
        rows = pl.ds(HALO + block * ROWS, ROWS)
        edge_out[0, block] = acc[rows, 0:PAD].astype(jnp.bfloat16)
        edge_out[1, block] = acc[rows, PAD + COLS : WIDE].astype(jnp.bfloat16)

        @pl.when(has_right)
        def _():
            grad_right(block, {"sky": sky + 1}).start()

        @pl.when(has_left)
        def _():
            grad_left(block, {"sky": sky - 1}).start()

    def merge_edges(block):
        rows = pl.ds(HALO + block * ROWS, ROWS)

        @pl.when(has_left)
        def _():
            grad_right(block, {"sky": sky - 1}).wait_recv()
            acc[rows, PAD : 2 * PAD] += edge_in[0, block].astype(jnp.float32)

        @pl.when(has_right)
        def _():
            grad_left(block, {"sky": sky + 1}).wait_recv()
            acc[rows, COLS : COLS + PAD] += edge_in[1, block].astype(jnp.float32)

    def reduce_down(block, part, where):
        rows = pl.ds(part * CHUNK, CHUNK)
        return remote(send_r.at[block, rows], recv_r.at[block, rows], rs_r_send.at[block, part], rs_r_recv.at[block, part], where)

    def reduce_up(block, part, where):
        rows = pl.ds(part * CHUNK, CHUNK)
        return remote(send_l.at[block, rows], recv_l.at[block, rows], rs_l_send.at[block, part], rs_l_recv.at[block, part], where)

    def pass_on(block, part, down):
        rows = pl.ds(part * CHUNK, CHUNK)
        mine = pl.ds(HALO + block * ROWS + part * CHUNK, CHUNK)
        staged, arrived = (send_r, recv_r) if down else (send_l, recv_l)
        move = reduce_down if down else reduce_up
        fed = has_up if down else has_down
        out_to = {"epoch": me + 1} if down else {"epoch": me - 1}
        in_from = {"epoch": me - 1} if down else {"epoch": me + 1}

        @pl.when(fed)
        def _():
            move(block, part, in_from).wait_recv()
            staged[block, rows] = (
                acc[mine, PAD : PAD + COLS] + arrived[block, rows].astype(jnp.float32)
            ).astype(jnp.bfloat16)

        @pl.when(jnp.logical_not(fed))
        def _():
            staged[block, rows] = acc[mine, PAD : PAD + COLS].astype(jnp.bfloat16)

        move(block, part, out_to).start()

    for block in order:
        merge_edges(block)
    for k in range(n - 1):
        down_block, up_block = n - 1 - k, k
        for part in range(PARTS):
            @pl.when(me < down_block)
            def _():
                pass_on(down_block, part, True)

            @pl.when(me > up_block)
            def _():
                pass_on(up_block, part, False)

    for part in range(PARTS):
        rows = pl.ds(part * CHUNK, CHUNK)
        mine = pl.ds(pl.multiple_of(HALO + me * ROWS + part * CHUNK, HALO), CHUNK)
        out_ref[rows, :] = acc[mine, PAD : PAD + COLS]

        @pl.when(has_up)
        def _():
            reduce_down(me, part, {"epoch": me - 1}).wait_recv()
            out_ref[rows, :] += recv_r[me, rows].astype(jnp.float32)

        @pl.when(has_down)
        def _():
            reduce_up(me, part, {"epoch": me + 1}).wait_recv()
            out_ref[rows, :] += recv_l[me, rows].astype(jnp.float32)

    for t in range(n - 1):
        for part in range(PARTS):
            @pl.when(has_down & (me - t >= 0))
            def _():
                gather_down(t, part).wait_send()

            @pl.when(has_up & (me + t <= n - 1))
            def _():
                gather_up(t, part).wait_send()

            @pl.when(me < n - 1 - t)
            def _():
                reduce_down(n - 1 - t, part, {"epoch": me + 1}).wait_send()

            @pl.when(me > t)
            def _():
                reduce_up(t, part, {"epoch": me - 1}).wait_send()
    for block in range(n):
        @pl.when(has_right)
        def _():
            sky_right(block).wait_send()
            grad_right(block, {"sky": sky + 1}).wait_send()

        @pl.when(has_left)
        def _():
            sky_left(block).wait_send()
            grad_left(block, {"sky": sky - 1}).wait_send()


def fused_plan(sky_scene, images, psf_rows, psf_cols, offsets, epoch_weight, column_mask, coverage):
    n, sky_count = lax.axis_size("epoch"), lax.axis_size("sky")
    local, total = images.shape[0], images.shape[1]
    taps = psf_rows.shape[1]
    psf = jnp.concatenate([psf_rows, psf_cols], axis=1).astype(jnp.float32)
    tile_column = lax.axis_index("sky") * COLS // TILE
    tiles = lax.dynamic_index_in_dim(coverage, tile_column, 2, keepdims=False)
    factor = 2.0 * epoch_weight[:, None] * tiles.astype(jnp.float32)
    bf, f32 = jnp.bfloat16, jnp.float32
    smem = pl.BlockSpec(memory_space=pltpu.SMEM)
    vmem = pl.BlockSpec(memory_space=pltpu.VMEM)
    anywhere = pl.BlockSpec(memory_space=pl.ANY)
    dma = pltpu.SemaphoreType.DMA
    return pl.pallas_call(
        functools.partial(fused_kernel, n, sky_count, taps, local),
        out_shape=jax.ShapeDtypeStruct((ROWS, COLS), f32),
        in_specs=[smem, smem, smem, vmem, anywhere, anywhere],
        out_specs=vmem,
        scratch_shapes=[
            pltpu.VMEM((total + 2 * HALO, WIDE), bf),
            pltpu.VMEM((total + 2 * HALO, WIDE), f32),
            pltpu.VMEM((local, total, COLS), bf),
            pltpu.VMEM((local, SUB, REACH), bf),
            pltpu.VMEM((REACH, local * SUB), bf),
            pltpu.VMEM((local, 512, 256), bf),
            pltpu.VMEM((CHUNK, WIDE), bf),
            pltpu.VMEM((CHUNK, COLS), bf),
            pltpu.VMEM((2, local * SUB, WIDE), bf),
            pltpu.VMEM((2, n, ROWS, PAD), bf),
            pltpu.VMEM((2, n, ROWS, PAD), bf),
            pltpu.VMEM((n, ROWS, COLS), bf),
            pltpu.VMEM((n, ROWS, COLS), bf),
            pltpu.VMEM((n, ROWS, COLS), bf),
            pltpu.VMEM((n, ROWS, COLS), bf),
            dma,
            dma((local,)),
        ]
        + [dma((n, PARTS))] * 4
        + [dma((n,))] * 4
        + [dma((n, PARTS))] * 4
        + [dma((n,))] * 4,
        compiler_params=pltpu.CompilerParams(
            collective_id=0, has_side_effects=True, vmem_limit_bytes=48 << 20
        ),
    )(psf, offsets, factor, column_mask, sky_scene, images)


def on_device(sky_scene, images, *rest):
    n = lax.axis_size("epoch")
    fits = (
        2 <= n <= 4
        and sky_scene.shape == (ROWS, COLS)
        and images.shape[1:] == (n * ROWS, COLS)
        and images.shape[0] <= 2
    )
    plan = fused_plan if fits else strip_plan
    return plan(sky_scene, images, *rest)


def solution(mesh):
    return jax.shard_map(
        on_device,
        mesh=mesh,
        in_specs=(
            P(("field", "epoch"), "sky"),
            P(("field", "epoch"), None, "sky"),
            P("field", None),
            P("field", None),
            P("field", None),
            P("field"),
            P("field", "sky"),
            P("field", None, None),
        ),
        out_specs=P(("field", "epoch"), "sky"),
        check_vma=False,
    )
```

```python
import functools
import jax
import jax.numpy as jnp
from jax import lax
from jax.experimental import pallas as pl
from jax.experimental.pallas import tpu as pltpu
from jax.sharding import PartitionSpec as P

TILE = 512
HALO = 16
MESH = pl.DeviceIdType.MESH
ROWS = 512
COLS = 512
PAD = 128
WIDE = COLS + 2 * PAD
SUB = 128
REACH = SUB + 2 * HALO
CHUNK = 256
PARTS = ROWS // CHUNK


def extended(value, sides, width):
    for axis, dim in sides:
        peers, length = (lax.axis_size(axis), value.shape[dim])
        up = [(i, (i + 1) % peers) for i in range(peers - 1)]
        down = [(j, i) for i, j in up]
        last = lax.slice_in_dim(value, length - width, length, axis=dim)
        initial = lax.slice_in_dim(value, 0, width, axis=dim)
        before = lax.ppermute(last, axis, up)
        after = lax.ppermute(initial, axis, down)
        value = jnp.concatenate([before, value, after], axis=dim)
    return value


def band_tables(kernels, shifts, count_in, count_out):
    row_index = lax.broadcasted_iota(jnp.int32, (count_in, count_out), 0)
    col_index = lax.broadcasted_iota(jnp.int32, (count_in, count_out), 1)
    spread = kernels.shape[1]
    half_width = (spread - 1) // 2
    position = (
        (row_index - col_index)[None]
        - shifts[:, None, None]
        + half_width
        - (count_in - count_out) // 2
    )
    band_table = jnp.zeros((kernels.shape[0], count_in, count_out), jnp.float32)
    for each_tap in range(spread):
        band_table = band_table + jnp.where(
            position == each_tap, kernels[:, each_tap, None, None].astype(jnp.float32), 0.0
        )
    return band_table.astype(jnp.bfloat16)


def epoch_block(window, row_table, col_table, image_block, factor):
    lifted = jnp.einsum("ki,kc->ic", row_table, window, preferred_element_type=jnp.float32).astype(
        jnp.bfloat16
    )
    modeled = jnp.dot(lifted, col_table, preferred_element_type=jnp.float32)
    residual = (factor * (modeled - image_block.astype(jnp.float32))).astype(jnp.bfloat16)
    pulled = jnp.einsum(
        "ic,kc->ik", residual, col_table, preferred_element_type=jnp.float32
    ).astype(jnp.bfloat16)
    return jnp.dot(row_table, pulled, preferred_element_type=jnp.float32)


def strip_plan(sky_scene, images, psf_rows, psf_cols, offsets, epoch_weight, column_mask, coverage):
    slab_cells = extended(sky_scene, (("sky", 1),), HALO)
    strip_cells = lax.all_gather(slab_cells, "epoch", axis=0, tiled=True)
    strip_cells = jnp.pad(strip_cells, ((HALO, HALO), (0, 0)))
    full_rows = strip_cells.shape[0] - 2 * HALO
    strip_width = sky_scene.shape[1]
    local_count = images.shape[0]
    epoch_base = lax.axis_index("epoch") * local_count
    tile_column = lax.axis_index("sky") * strip_width // TILE

    def per_epoch(local_epoch, running):
        epoch_now = epoch_base + local_epoch
        row_table = band_tables(
            psf_rows[epoch_now][None], offsets[epoch_now, 0][None], TILE + 2 * HALO, TILE
        )[0]
        col_table = band_tables(
            psf_cols[epoch_now][None],
            offsets[epoch_now, 1][None],
            strip_width + 2 * HALO,
            strip_width,
        )[0]
        observed = lax.dynamic_index_in_dim(images, local_epoch, 0, keepdims=False)
        weight = epoch_weight[epoch_now]
        mask_row = column_mask[epoch_now].astype(jnp.float32)
        for row_block in range(full_rows // TILE):
            covered_flag = coverage[epoch_now, row_block, tile_column]
            window = strip_cells[row_block * TILE : row_block * TILE + TILE + 2 * HALO]
            image_block = observed[row_block * TILE : (row_block + 1) * TILE]
            factor = 2.0 * weight * covered_flag.astype(jnp.float32) * mask_row

            def covered():
                return epoch_block(window, row_table, col_table, image_block, factor)

            def skipped():
                return jnp.zeros((TILE + 2 * HALO, strip_width + 2 * HALO), jnp.float32)

            grad_term = lax.cond(covered_flag > 0, covered, skipped)
            running = running.at[row_block * TILE : row_block * TILE + TILE + 2 * HALO].add(
                grad_term
            )
        return running

    running = lax.fori_loop(
        0,
        local_count,
        per_epoch,
        jnp.zeros((full_rows + 2 * HALO, strip_width + 2 * HALO), jnp.float32),
    )
    trimmed = running[HALO : HALO + full_rows]
    packed = jnp.concatenate([trimmed[:, :HALO], trimmed[:, strip_width + HALO :]], axis=1)
    center_raw = trimmed[:, HALO : HALO + strip_width]
    received = extended(packed, (("sky", 1),), HALO)
    center_cells = center_raw.at[:, :HALO].add(received[:, :HALO])
    center_cells = center_cells.at[:, strip_width - HALO :].add(received[:, 3 * HALO :])
    return lax.psum_scatter(center_cells, "epoch", scatter_dimension=0, tiled=True)


def band(position, psf_ref, epoch, first, taps):
    table = jnp.zeros(position.shape, jnp.float32)
    for tap in range(taps):
        table = jnp.where(position == tap, psf_ref[epoch, first + tap], table)
    return table.astype(jnp.bfloat16)


def fused_kernel(
    n, sky_count, taps, local,
    psf_ref, offset_ref, factor_ref, mask_ref, scene_ref, image_ref, out_ref,
    strip, acc, image_buf, row_tab, rowt_tab, col_tab, lift, res, pull,
    edge_out, edge_in, send_r, recv_r, send_l, recv_l,
    load_sem, image_sem,
    ag_r_send, ag_r_recv, ag_l_send, ag_l_recv,
    sky_r_send, sky_r_recv, sky_l_send, sky_l_recv,
    rs_r_send, rs_r_recv, rs_l_send, rs_l_recv,
    ed_r_send, ed_r_recv, ed_l_send, ed_l_recv,
):
    me = lax.axis_index("epoch")
    sky = lax.axis_index("sky")
    total = n * ROWS
    has_up, has_down = me > 0, me < n - 1
    has_left, has_right = sky > 0, sky < sky_count - 1
    base = me * local
    half = (taps - 1) // 2

    def rows_of(block, part=None):
        if part is None:
            return pl.ds(pl.multiple_of(HALO + block * ROWS, HALO), ROWS)
        return pl.ds(pl.multiple_of(HALO + block * ROWS + part * CHUNK, HALO), CHUNK)

    centre = pl.ds(PAD, COLS)
    load = pltpu.make_async_copy(scene_ref, strip.at[rows_of(me), centre], load_sem)
    load.start()
    image_loads = [
        pltpu.make_async_copy(image_ref.at[e], image_buf.at[e], image_sem.at[e])
        for e in range(local)
    ]

    barrier = pltpu.get_barrier_semaphore()
    greetings = (
        (has_up, {"epoch": me - 1}),
        (has_down, {"epoch": me + 1}),
        (has_left, {"sky": sky - 1}),
        (has_right, {"sky": sky + 1}),
    )
    for there, where in greetings:
        @pl.when(there)
        def _():
            pl.semaphore_signal(barrier, inc=1, device_id=where, device_id_type=MESH)
    pl.semaphore_wait(barrier, sum(there.astype(jnp.int32) for there, where in greetings))

    def remote(src, dst, ssem, rsem, where):
        return pltpu.make_async_remote_copy(
            src_ref=src, dst_ref=dst, send_sem=ssem, recv_sem=rsem,
            device_id=where, device_id_type=MESH,
        )

    def gather_down(t, part):
        piece = strip.at[rows_of(me - t, part), centre]
        return remote(piece, piece, ag_r_send.at[t, part], ag_r_recv.at[t, part], {"epoch": me + 1})

    def gather_down_in(t, part):
        piece = strip.at[rows_of(me - 1 - t, part), centre]
        return remote(piece, piece, ag_r_send.at[t, part], ag_r_recv.at[t, part], {"epoch": me - 1})

    def gather_up(t, part):
        piece = strip.at[rows_of(me + t, part), centre]
        return remote(piece, piece, ag_l_send.at[t, part], ag_l_recv.at[t, part], {"epoch": me - 1})

    def gather_up_in(t, part):
        piece = strip.at[rows_of(me + 1 + t, part), centre]
        return remote(piece, piece, ag_l_send.at[t, part], ag_l_recv.at[t, part], {"epoch": me + 1})

    def sky_right(block):
        return remote(
            strip.at[rows_of(block), pl.ds(COLS, PAD)], strip.at[rows_of(block), pl.ds(0, PAD)],
            sky_r_send.at[block], sky_r_recv.at[block], {"sky": sky + 1},
        )

    def sky_right_in(block):
        return remote(
            strip.at[rows_of(block), pl.ds(COLS, PAD)], strip.at[rows_of(block), pl.ds(0, PAD)],
            sky_r_send.at[block], sky_r_recv.at[block], {"sky": sky - 1},
        )

    def sky_left(block):
        return remote(
            strip.at[rows_of(block), pl.ds(PAD, PAD)], strip.at[rows_of(block), pl.ds(PAD + COLS, PAD)],
            sky_l_send.at[block], sky_l_recv.at[block], {"sky": sky - 1},
        )

    def sky_left_in(block):
        return remote(
            strip.at[rows_of(block), pl.ds(PAD, PAD)], strip.at[rows_of(block), pl.ds(PAD + COLS, PAD)],
            sky_l_send.at[block], sky_l_recv.at[block], {"sky": sky + 1},
        )

    def send_edges(block):
        @pl.when(has_right)
        def _():
            sky_right(block).start()

        @pl.when(has_left)
        def _():
            sky_left(block).start()

    def wait_edges(block):
        @pl.when(has_left)
        def _():
            sky_right_in(block).wait_recv()

        @pl.when(has_right)
        def _():
            sky_left_in(block).wait_recv()

    load.wait()
    for part in range(PARTS):
        @pl.when(has_down)
        def _():
            gather_down(0, part).start()

        @pl.when(has_up)
        def _():
            gather_up(0, part).start()
    send_edges(me)
    for copy in image_loads:
        copy.start()

    strip[pl.ds(0, HALO), :] = jnp.zeros((HALO, WIDE), jnp.bfloat16)
    strip[pl.ds(HALO + total, HALO), :] = jnp.zeros((HALO, WIDE), jnp.bfloat16)

    @pl.when(sky == 0)
    def _():
        strip[pl.ds(HALO, total), pl.ds(0, PAD)] = jnp.zeros((total, PAD), jnp.bfloat16)

    @pl.when(sky == sky_count - 1)
    def _():
        strip[pl.ds(HALO, total), pl.ds(PAD + COLS, PAD)] = jnp.zeros((total, PAD), jnp.bfloat16)

    def clear(i, carry):
        acc[pl.ds(pl.multiple_of(i * 32, 32), 32), :] = jnp.zeros((32, WIDE), jnp.float32)
        return carry

    lax.fori_loop(0, (total + 2 * HALO) // 32, clear, 0)

    for e in range(local):
        shift_r = offset_ref[base + e, 0]
        shift_c = offset_ref[base + e, 1]
        out_i = lax.broadcasted_iota(jnp.int32, (SUB, REACH), 0)
        in_i = lax.broadcasted_iota(jnp.int32, (SUB, REACH), 1)
        row_tab[e] = band(in_i - out_i - HALO - shift_r + half, psf_ref, base + e, 0, taps)
        in_t = lax.broadcasted_iota(jnp.int32, (REACH, SUB), 0)
        out_t = lax.broadcasted_iota(jnp.int32, (REACH, SUB), 1)
        rowt_tab[:, e * SUB : (e + 1) * SUB] = band(
            in_t - out_t - HALO - shift_r + half, psf_ref, base + e, 0, taps
        )

        def fill(i, carry):
            k = lax.broadcasted_iota(jnp.int32, (64, 256), 0) + i * 64
            j = lax.broadcasted_iota(jnp.int32, (64, 256), 1)
            col_tab[e, pl.ds(pl.multiple_of(i * 64, 64), 64), :] = band(
                k - j - PAD - shift_c + half, psf_ref, base + e, taps, taps
            )
            return carry

        lax.fori_loop(0, 8, fill, 0)

    def compute(q, carry):
        r0 = pl.multiple_of(q * CHUNK, CHUNK)
        for e in range(local):
            for u in range(2):
                window = strip[pl.ds(pl.multiple_of(r0 + u * SUB, SUB), REACH), :]
                lift[u * SUB : (u + 1) * SUB, :] = jnp.dot(
                    row_tab[e], window, preferred_element_type=jnp.float32
                ).astype(jnp.bfloat16)
            factor = factor_ref[base + e, q // PARTS] * mask_ref[pl.ds(base + e, 1), :].astype(
                jnp.float32
            )
            for h in range(2):
                cols = slice(h * 256, (h + 1) * 256)
                modeled = jnp.dot(
                    lift[:, h * 256 : h * 256 + 512], col_tab[e], preferred_element_type=jnp.float32
                )
                seen = image_buf[e, pl.ds(r0, CHUNK), cols].astype(jnp.float32)
                res[:, cols] = (factor[:, cols] * (modeled - seen)).astype(jnp.bfloat16)

            def back(h, side):
                return lax.dot_general(
                    res[:, h * 256 : (h + 1) * 256],
                    col_tab[e, side * 256 : (side + 1) * 256, :],
                    (((1,), (1,)), ((), ())),
                    preferred_element_type=jnp.float32,
                )

            pulls = (back(0, 0), back(0, 1) + back(1, 0), back(1, 1))
            for third, value in enumerate(pulls):
                narrow = value.astype(jnp.bfloat16)
                for u in range(2):
                    pull[u, e * SUB : (e + 1) * SUB, third * 256 : (third + 1) * 256] = narrow[
                        u * SUB : (u + 1) * SUB
                    ]
        for u in range(2):
            where = pl.ds(pl.multiple_of(r0 + u * SUB, SUB), REACH)
            acc[where, :] += jnp.dot(rowt_tab[...], pull[u], preferred_element_type=jnp.float32)
        return carry

    for copy in image_loads:
        copy.wait()
    wait_edges(me)

    upper = me < n // 2
    near_low = jnp.where(upper, 0, n // 2)

    def ready(t):
        low = jnp.maximum(me - t, 0)
        high = jnp.minimum(me + t, n - 1)
        first = jnp.where(low == 0, 0, low + 1)
        stop = jnp.where(high == n - 1, n, high)
        return jnp.maximum(first, near_low), jnp.minimum(stop, near_low + n // 2)

    for t in range(n - 1):
        for part in range(PARTS):
            @pl.when(me - 1 - t >= 0)
            def _():
                gather_down_in(t, part).wait_recv()
                if t + 1 < n - 1:
                    @pl.when(has_down)
                    def _():
                        gather_down(t + 1, part).start()

            @pl.when(me + 1 + t <= n - 1)
            def _():
                gather_up_in(t, part).wait_recv()
                if t + 1 < n - 1:
                    @pl.when(has_up)
                    def _():
                        gather_up(t + 1, part).start()

        @pl.when(me - 1 - t >= 0)
        def _():
            send_edges(me - 1 - t)

        @pl.when(me + 1 + t <= n - 1)
        def _():
            send_edges(me + 1 + t)

        @pl.when(me - 1 - t >= 0)
        def _():
            wait_edges(me - 1 - t)

        @pl.when(me + 1 + t <= n - 1)
        def _():
            wait_edges(me + 1 + t)

        first, stop = ready(t + 1)
        if t == 0:
            lax.fori_loop(first * PARTS, stop * PARTS, compute, 0)
        elif t == 1:
            @pl.when((me == 0) | (me == n - 1))
            def _():
                block = jnp.where(upper, 1, n - 2)
                lax.fori_loop(block * PARTS, (block + 1) * PARTS, compute, 0)

    pieces = n * PARTS
    half_pieces = pieces // 2

    def far(i):
        return jnp.where(upper, pieces - 1 - i, i)

    def near(j):
        return jnp.where(upper, j, pieces - 1 - j)

    def flat(q):
        return pl.ds(pl.multiple_of(q * CHUNK, CHUNK), CHUNK)

    def mine(q):
        return pl.ds(pl.multiple_of(HALO + q * CHUNK, HALO), CHUNK)

    def grad_right(q, where):
        return remote(edge_out.at[1, flat(q)], edge_in.at[0, flat(q)], ed_r_send.at[q], ed_r_recv.at[q], where)

    def grad_left(q, where):
        return remote(edge_out.at[0, flat(q)], edge_in.at[1, flat(q)], ed_l_send.at[q], ed_l_recv.at[q], where)

    def share(q):
        @pl.when(has_right)
        def _():
            edge_out[1, flat(q), :] = acc[mine(q), PAD + COLS : WIDE].astype(jnp.bfloat16)
            grad_right(q, {"sky": sky + 1}).start()

        @pl.when(has_left)
        def _():
            edge_out[0, flat(q), :] = acc[mine(q), 0:PAD].astype(jnp.bfloat16)
            grad_left(q, {"sky": sky - 1}).start()

    def merge(q):
        @pl.when(has_left)
        def _():
            grad_right(q, {"sky": sky - 1}).wait_recv()
            acc[mine(q), PAD : 2 * PAD] += edge_in[0, flat(q), :].astype(jnp.float32)

        @pl.when(has_right)
        def _():
            grad_left(q, {"sky": sky + 1}).wait_recv()
            acc[mine(q), COLS : COLS + PAD] += edge_in[1, flat(q), :].astype(jnp.float32)

    def reduce_down(q, where):
        return remote(send_r.at[flat(q)], recv_r.at[flat(q)], rs_r_send.at[q], rs_r_recv.at[q], where)

    def reduce_up(q, where):
        return remote(send_l.at[flat(q)], recv_l.at[flat(q)], rs_l_send.at[q], rs_l_recv.at[q], where)

    def pass_on(q, down):
        staged, arrived = (send_r, recv_r) if down else (send_l, recv_l)
        move = reduce_down if down else reduce_up
        fed = has_up if down else has_down
        out_to = {"epoch": me + 1} if down else {"epoch": me - 1}
        in_from = {"epoch": me - 1} if down else {"epoch": me + 1}

        @pl.when(fed)
        def _():
            move(q, in_from).wait_recv()
            staged[flat(q), :] = (
                acc[mine(q), PAD : PAD + COLS] + arrived[flat(q), :].astype(jnp.float32)
            ).astype(jnp.bfloat16)

        @pl.when(jnp.logical_not(fed))
        def _():
            staged[flat(q), :] = acc[mine(q), PAD : PAD + COLS].astype(jnp.bfloat16)

        move(q, out_to).start()

    def pass_far(i):
        merge(far(i))

        @pl.when(upper)
        def _():
            pass_on(far(i), True)

        @pl.when(jnp.logical_not(upper))
        def _():
            pass_on(far(i), False)

    inner = (me > 0) & (me < n - 1)

    def pass_near(j):
        merge(near(j))
        inward = upper != inner

        @pl.when(inward)
        def _():
            pass_on(near(j), True)

        @pl.when(jnp.logical_not(inward))
        def _():
            pass_on(near(j), False)

    for j in range(half_pieces - 1):
        share(near(j))
    for i in range(half_pieces):
        compute(far(i), 0)
        if i >= 1:
            share(far(i - 1))
        if i >= 2:
            pass_far(i - 2)
    share(far(half_pieces - 1))
    share(near(half_pieces - 1))
    for i in range(half_pieces - 2, PARTS):
        pass_far(i)

    @pl.when(inner)
    def _():
        for j in range(PARTS):
            pass_near(j)

    for i in range(max(PARTS, half_pieces - 2), half_pieces):
        pass_far(i)

    @pl.when(jnp.logical_not(inner))
    def _():
        for j in range(PARTS, half_pieces):
            pass_near(j)

    for part in range(PARTS):
        rows = pl.ds(part * CHUNK, CHUNK)
        q = me * PARTS + part
        merge(q)
        out_ref[rows, :] = acc[mine(q), PAD : PAD + COLS]

        @pl.when(has_up)
        def _():
            reduce_down(q, {"epoch": me - 1}).wait_recv()
            out_ref[rows, :] += recv_r[flat(q), :].astype(jnp.float32)

        @pl.when(has_down)
        def _():
            reduce_up(q, {"epoch": me + 1}).wait_recv()
            out_ref[rows, :] += recv_l[flat(q), :].astype(jnp.float32)

    for t in range(n - 1):
        for part in range(PARTS):
            @pl.when(has_down & (me - t >= 0))
            def _():
                gather_down(t, part).wait_send()

            @pl.when(has_up & (me + t <= n - 1))
            def _():
                gather_up(t, part).wait_send()
    for q in range(pieces):
        @pl.when(me < q // PARTS)
        def _():
            reduce_down(q, {"epoch": me + 1}).wait_send()

        @pl.when(me > q // PARTS)
        def _():
            reduce_up(q, {"epoch": me - 1}).wait_send()

        @pl.when(has_right)
        def _():
            grad_right(q, {"sky": sky + 1}).wait_send()

        @pl.when(has_left)
        def _():
            grad_left(q, {"sky": sky - 1}).wait_send()
    for block in range(n):
        @pl.when(has_right)
        def _():
            sky_right(block).wait_send()

        @pl.when(has_left)
        def _():
            sky_left(block).wait_send()


def fused_plan(sky_scene, images, psf_rows, psf_cols, offsets, epoch_weight, column_mask, coverage):
    n, sky_count = lax.axis_size("epoch"), lax.axis_size("sky")
    local, total = images.shape[0], images.shape[1]
    taps = psf_rows.shape[1]
    psf = jnp.concatenate([psf_rows, psf_cols], axis=1).astype(jnp.float32)
    tile_column = lax.axis_index("sky") * COLS // TILE
    tiles = lax.dynamic_index_in_dim(coverage, tile_column, 2, keepdims=False)
    factor = 2.0 * epoch_weight[:, None] * tiles.astype(jnp.float32)
    bf, f32 = jnp.bfloat16, jnp.float32
    smem = pl.BlockSpec(memory_space=pltpu.SMEM)
    vmem = pl.BlockSpec(memory_space=pltpu.VMEM)
    anywhere = pl.BlockSpec(memory_space=pl.ANY)
    dma = pltpu.SemaphoreType.DMA
    return pl.pallas_call(
        functools.partial(fused_kernel, n, sky_count, taps, local),
        out_shape=jax.ShapeDtypeStruct((ROWS, COLS), f32),
        in_specs=[smem, smem, smem, vmem, anywhere, anywhere],
        out_specs=vmem,
        scratch_shapes=[
            pltpu.VMEM((total + 2 * HALO, WIDE), bf),
            pltpu.VMEM((total + 2 * HALO, WIDE), f32),
            pltpu.VMEM((local, total, COLS), bf),
            pltpu.VMEM((local, SUB, REACH), bf),
            pltpu.VMEM((REACH, local * SUB), bf),
            pltpu.VMEM((local, 512, 256), bf),
            pltpu.VMEM((CHUNK, WIDE), bf),
            pltpu.VMEM((CHUNK, COLS), bf),
            pltpu.VMEM((2, local * SUB, WIDE), bf),
            pltpu.VMEM((2, total, PAD), bf),
            pltpu.VMEM((2, total, PAD), bf),
            pltpu.VMEM((total, COLS), bf),
            pltpu.VMEM((total, COLS), bf),
            pltpu.VMEM((total, COLS), bf),
            pltpu.VMEM((total, COLS), bf),
            dma,
            dma((local,)),
        ]
        + [dma((n, PARTS))] * 4
        + [dma((n,))] * 4
        + [dma((n * PARTS,))] * 8,
        compiler_params=pltpu.CompilerParams(
            collective_id=0, has_side_effects=True, vmem_limit_bytes=48 << 20
        ),
    )(psf, offsets, factor, column_mask, sky_scene, images)


def on_device(sky_scene, images, *rest):
    n = lax.axis_size("epoch")
    fits = (
        n == 4
        and sky_scene.shape == (ROWS, COLS)
        and images.shape[1:] == (n * ROWS, COLS)
        and images.shape[0] <= 2
    )
    plan = fused_plan if fits else strip_plan
    return plan(sky_scene, images, *rest)


def solution(mesh):
    return jax.shard_map(
        on_device,
        mesh=mesh,
        in_specs=(
            P(("field", "epoch"), "sky"),
            P(("field", "epoch"), None, "sky"),
            P("field", None),
            P("field", None),
            P("field", None),
            P("field"),
            P("field", "sky"),
            P("field", None, None),
        ),
        out_specs=P(("field", "epoch"), "sky"),
        check_vma=False,
    )
```

```python
import functools
import jax
import jax.numpy as jnp
from jax import lax
from jax.experimental import pallas as pl
from jax.experimental.pallas import tpu as pltpu
from jax.sharding import PartitionSpec as P

TILE = 512
HALO = 16
MESH = pl.DeviceIdType.MESH
ROWS = 512
COLS = 512
PAD = 128
WIDE = COLS + 2 * PAD
SUB = 128
REACH = SUB + 2 * HALO
CHUNK = 256
PARTS = ROWS // CHUNK


def extended(value, sides, width):
    for axis, dim in sides:
        peers, length = (lax.axis_size(axis), value.shape[dim])
        up = [(i, (i + 1) % peers) for i in range(peers - 1)]
        down = [(j, i) for i, j in up]
        last = lax.slice_in_dim(value, length - width, length, axis=dim)
        initial = lax.slice_in_dim(value, 0, width, axis=dim)
        before = lax.ppermute(last, axis, up)
        after = lax.ppermute(initial, axis, down)
        value = jnp.concatenate([before, value, after], axis=dim)
    return value


def band_tables(kernels, shifts, count_in, count_out):
    row_index = lax.broadcasted_iota(jnp.int32, (count_in, count_out), 0)
    col_index = lax.broadcasted_iota(jnp.int32, (count_in, count_out), 1)
    spread = kernels.shape[1]
    half_width = (spread - 1) // 2
    position = (
        (row_index - col_index)[None]
        - shifts[:, None, None]
        + half_width
        - (count_in - count_out) // 2
    )
    band_table = jnp.zeros((kernels.shape[0], count_in, count_out), jnp.float32)
    for each_tap in range(spread):
        band_table = band_table + jnp.where(
            position == each_tap, kernels[:, each_tap, None, None].astype(jnp.float32), 0.0
        )
    return band_table.astype(jnp.bfloat16)


def epoch_block(window, row_table, col_table, image_block, factor):
    lifted = jnp.einsum("ki,kc->ic", row_table, window, preferred_element_type=jnp.float32).astype(
        jnp.bfloat16
    )
    modeled = jnp.dot(lifted, col_table, preferred_element_type=jnp.float32)
    residual = (factor * (modeled - image_block.astype(jnp.float32))).astype(jnp.bfloat16)
    pulled = jnp.einsum(
        "ic,kc->ik", residual, col_table, preferred_element_type=jnp.float32
    ).astype(jnp.bfloat16)
    return jnp.dot(row_table, pulled, preferred_element_type=jnp.float32)


def strip_plan(sky_scene, images, psf_rows, psf_cols, offsets, epoch_weight, column_mask, coverage):
    slab_cells = extended(sky_scene, (("sky", 1),), HALO)
    strip_cells = lax.all_gather(slab_cells, "epoch", axis=0, tiled=True)
    strip_cells = jnp.pad(strip_cells, ((HALO, HALO), (0, 0)))
    full_rows = strip_cells.shape[0] - 2 * HALO
    strip_width = sky_scene.shape[1]
    local_count = images.shape[0]
    epoch_base = lax.axis_index("epoch") * local_count
    tile_column = lax.axis_index("sky") * strip_width // TILE

    def per_epoch(local_epoch, running):
        epoch_now = epoch_base + local_epoch
        row_table = band_tables(
            psf_rows[epoch_now][None], offsets[epoch_now, 0][None], TILE + 2 * HALO, TILE
        )[0]
        col_table = band_tables(
            psf_cols[epoch_now][None],
            offsets[epoch_now, 1][None],
            strip_width + 2 * HALO,
            strip_width,
        )[0]
        observed = lax.dynamic_index_in_dim(images, local_epoch, 0, keepdims=False)
        weight = epoch_weight[epoch_now]
        mask_row = column_mask[epoch_now].astype(jnp.float32)
        for row_block in range(full_rows // TILE):
            covered_flag = coverage[epoch_now, row_block, tile_column]
            window = strip_cells[row_block * TILE : row_block * TILE + TILE + 2 * HALO]
            image_block = observed[row_block * TILE : (row_block + 1) * TILE]
            factor = 2.0 * weight * covered_flag.astype(jnp.float32) * mask_row

            def covered():
                return epoch_block(window, row_table, col_table, image_block, factor)

            def skipped():
                return jnp.zeros((TILE + 2 * HALO, strip_width + 2 * HALO), jnp.float32)

            grad_term = lax.cond(covered_flag > 0, covered, skipped)
            running = running.at[row_block * TILE : row_block * TILE + TILE + 2 * HALO].add(
                grad_term
            )
        return running

    running = lax.fori_loop(
        0,
        local_count,
        per_epoch,
        jnp.zeros((full_rows + 2 * HALO, strip_width + 2 * HALO), jnp.float32),
    )
    trimmed = running[HALO : HALO + full_rows]
    packed = jnp.concatenate([trimmed[:, :HALO], trimmed[:, strip_width + HALO :]], axis=1)
    center_raw = trimmed[:, HALO : HALO + strip_width]
    received = extended(packed, (("sky", 1),), HALO)
    center_cells = center_raw.at[:, :HALO].add(received[:, :HALO])
    center_cells = center_cells.at[:, strip_width - HALO :].add(received[:, 3 * HALO :])
    return lax.psum_scatter(center_cells, "epoch", scatter_dimension=0, tiled=True)


def band(position, psf_ref, epoch, first, taps):
    table = jnp.zeros(position.shape, jnp.float32)
    for tap in range(taps):
        table = jnp.where(position == tap, psf_ref[epoch, first + tap], table)
    return table.astype(jnp.bfloat16)


def fused_kernel(
    n, sky_count, taps, local,
    psf_ref, mask_in, scene_ref, image_ref, out_ref,
    strip, acc, image_buf, mask_ref, row_tab, rowt_tab, col_tab, lift, res, pull,
    edge_out, edge_in, send_r, recv_r, send_l, recv_l,
    load_sem, image_sem, mask_sem,
    ag_r_send, ag_r_recv, ag_l_send, ag_l_recv,
    sky_r_send, sky_r_recv, sky_l_send, sky_l_recv,
    rs_r_send, rs_r_recv, rs_l_send, rs_l_recv,
    ed_r_send, ed_r_recv, ed_l_send, ed_l_recv,
):
    me = lax.axis_index("epoch")
    sky = lax.axis_index("sky")
    total = n * ROWS
    has_up, has_down = me > 0, me < n - 1
    has_left, has_right = sky > 0, sky < sky_count - 1
    base = me * local
    half = (taps - 1) // 2

    def rows_of(block, part=None):
        if part is None:
            return pl.ds(pl.multiple_of(HALO + block * ROWS, HALO), ROWS)
        return pl.ds(pl.multiple_of(HALO + block * ROWS + part * CHUNK, HALO), CHUNK)

    centre = pl.ds(PAD, COLS)
    load = pltpu.make_async_copy(scene_ref, strip.at[rows_of(me), centre], load_sem)
    load.start()
    mask_load = pltpu.make_async_copy(mask_in, mask_ref, mask_sem)
    mask_load.start()
    image_loads = [
        pltpu.make_async_copy(image_ref.at[e], image_buf.at[e], image_sem.at[e])
        for e in range(local)
    ]

    barrier = pltpu.get_barrier_semaphore()
    greetings = (
        (has_up, {"epoch": me - 1}),
        (has_down, {"epoch": me + 1}),
        (has_left, {"sky": sky - 1}),
        (has_right, {"sky": sky + 1}),
    )
    for there, where in greetings:
        @pl.when(there)
        def _():
            pl.semaphore_signal(barrier, inc=1, device_id=where, device_id_type=MESH)
    pl.semaphore_wait(barrier, sum(there.astype(jnp.int32) for there, where in greetings))

    def remote(src, dst, ssem, rsem, where):
        return pltpu.make_async_remote_copy(
            src_ref=src, dst_ref=dst, send_sem=ssem, recv_sem=rsem,
            device_id=where, device_id_type=MESH,
        )

    def gather_down(t, part):
        piece = strip.at[rows_of(me - t, part), centre]
        return remote(piece, piece, ag_r_send.at[t, part], ag_r_recv.at[t, part], {"epoch": me + 1})

    def gather_down_in(t, part):
        piece = strip.at[rows_of(me - 1 - t, part), centre]
        return remote(piece, piece, ag_r_send.at[t, part], ag_r_recv.at[t, part], {"epoch": me - 1})

    def gather_up(t, part):
        piece = strip.at[rows_of(me + t, part), centre]
        return remote(piece, piece, ag_l_send.at[t, part], ag_l_recv.at[t, part], {"epoch": me - 1})

    def gather_up_in(t, part):
        piece = strip.at[rows_of(me + 1 + t, part), centre]
        return remote(piece, piece, ag_l_send.at[t, part], ag_l_recv.at[t, part], {"epoch": me + 1})

    def sky_right(block):
        return remote(
            strip.at[rows_of(block), pl.ds(COLS, PAD)], strip.at[rows_of(block), pl.ds(0, PAD)],
            sky_r_send.at[block], sky_r_recv.at[block], {"sky": sky + 1},
        )

    def sky_right_in(block):
        return remote(
            strip.at[rows_of(block), pl.ds(COLS, PAD)], strip.at[rows_of(block), pl.ds(0, PAD)],
            sky_r_send.at[block], sky_r_recv.at[block], {"sky": sky - 1},
        )

    def sky_left(block):
        return remote(
            strip.at[rows_of(block), pl.ds(PAD, PAD)], strip.at[rows_of(block), pl.ds(PAD + COLS, PAD)],
            sky_l_send.at[block], sky_l_recv.at[block], {"sky": sky - 1},
        )

    def sky_left_in(block):
        return remote(
            strip.at[rows_of(block), pl.ds(PAD, PAD)], strip.at[rows_of(block), pl.ds(PAD + COLS, PAD)],
            sky_l_send.at[block], sky_l_recv.at[block], {"sky": sky + 1},
        )

    def send_edges(block):
        @pl.when(has_right)
        def _():
            sky_right(block).start()

        @pl.when(has_left)
        def _():
            sky_left(block).start()

    def wait_edges(block):
        @pl.when(has_left)
        def _():
            sky_right_in(block).wait_recv()

        @pl.when(has_right)
        def _():
            sky_left_in(block).wait_recv()

    load.wait()
    for part in range(PARTS):
        @pl.when(has_down)
        def _():
            gather_down(0, part).start()

        @pl.when(has_up)
        def _():
            gather_up(0, part).start()
    send_edges(me)
    for copy in image_loads:
        copy.start()

    strip[pl.ds(0, HALO), :] = jnp.zeros((HALO, WIDE), jnp.bfloat16)
    strip[pl.ds(HALO + total, HALO), :] = jnp.zeros((HALO, WIDE), jnp.bfloat16)

    @pl.when(sky == 0)
    def _():
        strip[pl.ds(HALO, total), pl.ds(0, PAD)] = jnp.zeros((total, PAD), jnp.bfloat16)

    @pl.when(sky == sky_count - 1)
    def _():
        strip[pl.ds(HALO, total), pl.ds(PAD + COLS, PAD)] = jnp.zeros((total, PAD), jnp.bfloat16)

    def clear(i, carry):
        acc[pl.ds(pl.multiple_of(i * 32, 32), 32), :] = jnp.zeros((32, WIDE), jnp.float32)
        return carry

    lax.fori_loop(0, (total + 2 * HALO) // 32, clear, 0)

    for e in range(local):
        shift_r = psf_ref[base + e, 2 * taps].astype(jnp.int32)
        shift_c = psf_ref[base + e, 2 * taps + 1].astype(jnp.int32)
        out_i = lax.broadcasted_iota(jnp.int32, (SUB, REACH), 0)
        in_i = lax.broadcasted_iota(jnp.int32, (SUB, REACH), 1)
        row_tab[e] = band(in_i - out_i - HALO - shift_r + half, psf_ref, base + e, 0, taps)
        in_t = lax.broadcasted_iota(jnp.int32, (REACH, SUB), 0)
        out_t = lax.broadcasted_iota(jnp.int32, (REACH, SUB), 1)
        rowt_tab[:, e * SUB : (e + 1) * SUB] = band(
            in_t - out_t - HALO - shift_r + half, psf_ref, base + e, 0, taps
        )

        def fill(i, carry):
            k = lax.broadcasted_iota(jnp.int32, (64, 256), 0) + i * 64
            j = lax.broadcasted_iota(jnp.int32, (64, 256), 1)
            col_tab[e, pl.ds(pl.multiple_of(i * 64, 64), 64), :] = band(
                k - j - PAD - shift_c + half, psf_ref, base + e, taps, taps
            )
            return carry

        lax.fori_loop(0, 8, fill, 0)

    def compute(q, carry):
        r0 = pl.multiple_of(q * CHUNK, CHUNK)
        for e in range(local):
            for u in range(2):
                window = strip[pl.ds(pl.multiple_of(r0 + u * SUB, SUB), REACH), :]
                lift[u * SUB : (u + 1) * SUB, :] = jnp.dot(
                    row_tab[e], window, preferred_element_type=jnp.float32
                ).astype(jnp.bfloat16)
            factor = psf_ref[base + e, 2 * taps + 2 + q // PARTS] * mask_ref[pl.ds(base + e, 1), :].astype(
                jnp.float32
            )
            for h in range(2):
                cols = slice(h * 256, (h + 1) * 256)
                modeled = jnp.dot(
                    lift[:, h * 256 : h * 256 + 512], col_tab[e], preferred_element_type=jnp.float32
                )
                seen = image_buf[e, pl.ds(r0, CHUNK), cols].astype(jnp.float32)
                res[:, cols] = (factor[:, cols] * (modeled - seen)).astype(jnp.bfloat16)

            def back(h, side):
                return lax.dot_general(
                    res[:, h * 256 : (h + 1) * 256],
                    col_tab[e, side * 256 : (side + 1) * 256, :],
                    (((1,), (1,)), ((), ())),
                    preferred_element_type=jnp.float32,
                )

            pulls = (back(0, 0), back(0, 1) + back(1, 0), back(1, 1))
            for third, value in enumerate(pulls):
                narrow = value.astype(jnp.bfloat16)
                for u in range(2):
                    pull[u, e * SUB : (e + 1) * SUB, third * 256 : (third + 1) * 256] = narrow[
                        u * SUB : (u + 1) * SUB
                    ]
        for u in range(2):
            where = pl.ds(pl.multiple_of(r0 + u * SUB, SUB), REACH)
            acc[where, :] += jnp.dot(rowt_tab[...], pull[u], preferred_element_type=jnp.float32)
        return carry

    mask_load.wait()
    for copy in image_loads:
        copy.wait()
    wait_edges(me)

    upper = me < n // 2
    near_low = jnp.where(upper, 0, n // 2)

    def ready(t):
        low = jnp.maximum(me - t, 0)
        high = jnp.minimum(me + t, n - 1)
        first = jnp.where(low == 0, 0, low + 1)
        stop = jnp.where(high == n - 1, n, high)
        return jnp.maximum(first, near_low), jnp.minimum(stop, near_low + n // 2)

    pieces = n * PARTS
    half_pieces = pieces // 2

    def far(i):
        return jnp.where(upper, pieces - 1 - i, i)

    def near(j):
        return jnp.where(upper, j, pieces - 1 - j)

    def flat(q):
        return pl.ds(pl.multiple_of(q * CHUNK, CHUNK), CHUNK)

    def mine(q):
        return pl.ds(pl.multiple_of(HALO + q * CHUNK, HALO), CHUNK)

    def grad_right(q, where):
        return remote(edge_out.at[1, flat(q)], edge_in.at[0, flat(q)], ed_r_send.at[q], ed_r_recv.at[q], where)

    def grad_left(q, where):
        return remote(edge_out.at[0, flat(q)], edge_in.at[1, flat(q)], ed_l_send.at[q], ed_l_recv.at[q], where)

    def share(q):
        @pl.when(has_right)
        def _():
            edge_out[1, flat(q), :] = acc[mine(q), PAD + COLS : WIDE].astype(jnp.bfloat16)
            grad_right(q, {"sky": sky + 1}).start()

        @pl.when(has_left)
        def _():
            edge_out[0, flat(q), :] = acc[mine(q), 0:PAD].astype(jnp.bfloat16)
            grad_left(q, {"sky": sky - 1}).start()

    def merge(q):
        @pl.when(has_left)
        def _():
            grad_right(q, {"sky": sky - 1}).wait_recv()
            acc[mine(q), PAD : 2 * PAD] += edge_in[0, flat(q), :].astype(jnp.float32)

        @pl.when(has_right)
        def _():
            grad_left(q, {"sky": sky + 1}).wait_recv()
            acc[mine(q), COLS : COLS + PAD] += edge_in[1, flat(q), :].astype(jnp.float32)

    def reduce_down(q, where):
        return remote(send_r.at[flat(q)], recv_r.at[flat(q)], rs_r_send.at[q], rs_r_recv.at[q], where)

    def reduce_up(q, where):
        return remote(send_l.at[flat(q)], recv_l.at[flat(q)], rs_l_send.at[q], rs_l_recv.at[q], where)

    def pass_on(q, down):
        staged, arrived = (send_r, recv_r) if down else (send_l, recv_l)
        move = reduce_down if down else reduce_up
        fed = has_up if down else has_down
        out_to = {"epoch": me + 1} if down else {"epoch": me - 1}
        in_from = {"epoch": me - 1} if down else {"epoch": me + 1}

        @pl.when(fed)
        def _():
            move(q, in_from).wait_recv()
            staged[flat(q), :] = (
                acc[mine(q), PAD : PAD + COLS] + arrived[flat(q), :].astype(jnp.float32)
            ).astype(jnp.bfloat16)

        @pl.when(jnp.logical_not(fed))
        def _():
            staged[flat(q), :] = acc[mine(q), PAD : PAD + COLS].astype(jnp.bfloat16)

        move(q, out_to).start()

    def pass_far(i):
        merge(far(i))

        @pl.when(upper)
        def _():
            pass_on(far(i), True)

        @pl.when(jnp.logical_not(upper))
        def _():
            pass_on(far(i), False)

    inner = (me > 0) & (me < n - 1)

    def pass_near(j):
        merge(near(j))
        inward = upper != inner

        @pl.when(inward)
        def _():
            pass_on(near(j), True)

        @pl.when(jnp.logical_not(inward))
        def _():
            pass_on(near(j), False)

    for t in range(n - 1):
        for part in range(PARTS):
            @pl.when(me - 1 - t >= 0)
            def _():
                gather_down_in(t, part).wait_recv()
                if t + 1 < n - 1:
                    @pl.when(has_down)
                    def _():
                        gather_down(t + 1, part).start()

            @pl.when(me + 1 + t <= n - 1)
            def _():
                gather_up_in(t, part).wait_recv()
                if t + 1 < n - 1:
                    @pl.when(has_up)
                    def _():
                        gather_up(t + 1, part).start()

        @pl.when(me - 1 - t >= 0)
        def _():
            send_edges(me - 1 - t)

        @pl.when(me + 1 + t <= n - 1)
        def _():
            send_edges(me + 1 + t)

        @pl.when(me - 1 - t >= 0)
        def _():
            wait_edges(me - 1 - t)

        @pl.when(me + 1 + t <= n - 1)
        def _():
            wait_edges(me + 1 + t)

        first, stop = ready(t + 1)
        if t == 0:
            lax.fori_loop(first * PARTS, stop * PARTS, compute, 0)
        elif t == 1:
            @pl.when((me == 0) | (me == n - 1))
            def _():
                block = jnp.where(upper, 1, n - 2)
                lax.fori_loop(block * PARTS, (block + 1) * PARTS, compute, 0)
                for j in range(half_pieces - 1):
                    share(near(j))
                compute(far(half_pieces - 1), 0)
                share(near(half_pieces - 1))
                for j in range(PARTS, half_pieces):
                    pass_near(j)

    @pl.when(inner)
    def _():
        for j in range(half_pieces - 1):
            share(near(j))

    for i in range(half_pieces):
        if i < half_pieces - 1:
            compute(far(i), 0)
        else:
            @pl.when(inner)
            def _():
                compute(far(i), 0)
        if i >= 1:
            share(far(i - 1))
        if i >= 2:
            pass_far(i - 2)
    share(far(half_pieces - 1))

    @pl.when(inner)
    def _():
        share(near(half_pieces - 1))

    for i in range(half_pieces - 2, PARTS):
        pass_far(i)

    @pl.when(inner)
    def _():
        for j in range(PARTS):
            pass_near(j)

    for i in range(max(PARTS, half_pieces - 2), half_pieces):
        pass_far(i)

    for part in range(PARTS):
        rows = pl.ds(part * CHUNK, CHUNK)
        q = me * PARTS + part
        merge(q)
        out_ref[rows, :] = acc[mine(q), PAD : PAD + COLS]

        @pl.when(has_up)
        def _():
            reduce_down(q, {"epoch": me - 1}).wait_recv()
            out_ref[rows, :] += recv_r[flat(q), :].astype(jnp.float32)

        @pl.when(has_down)
        def _():
            reduce_up(q, {"epoch": me + 1}).wait_recv()
            out_ref[rows, :] += recv_l[flat(q), :].astype(jnp.float32)

    for t in range(n - 1):
        for part in range(PARTS):
            @pl.when(has_down & (me - t >= 0))
            def _():
                gather_down(t, part).wait_send()

            @pl.when(has_up & (me + t <= n - 1))
            def _():
                gather_up(t, part).wait_send()
    for q in range(pieces):
        @pl.when(me < q // PARTS)
        def _():
            reduce_down(q, {"epoch": me + 1}).wait_send()

        @pl.when(me > q // PARTS)
        def _():
            reduce_up(q, {"epoch": me - 1}).wait_send()

        @pl.when(has_right)
        def _():
            grad_right(q, {"sky": sky + 1}).wait_send()

        @pl.when(has_left)
        def _():
            grad_left(q, {"sky": sky - 1}).wait_send()
    for block in range(n):
        @pl.when(has_right)
        def _():
            sky_right(block).wait_send()

        @pl.when(has_left)
        def _():
            sky_left(block).wait_send()


def fused_plan(sky_scene, images, psf_rows, psf_cols, offsets, epoch_weight, column_mask, coverage):
    n, sky_count = lax.axis_size("epoch"), lax.axis_size("sky")
    local, total = images.shape[0], images.shape[1]
    taps = psf_rows.shape[1]
    tile_column = lax.axis_index("sky") * COLS // TILE
    tiles = lax.dynamic_index_in_dim(coverage, tile_column, 2, keepdims=False)
    factor = 2.0 * epoch_weight[:, None] * tiles.astype(jnp.float32)
    bf, f32 = jnp.bfloat16, jnp.float32
    scalars = jnp.concatenate(
        [value.astype(f32) for value in (psf_rows, psf_cols, offsets, factor)], axis=1
    )
    smem = pl.BlockSpec(memory_space=pltpu.SMEM)
    vmem = pl.BlockSpec(memory_space=pltpu.VMEM)
    anywhere = pl.BlockSpec(memory_space=pl.ANY)
    dma = pltpu.SemaphoreType.DMA
    return pl.pallas_call(
        functools.partial(fused_kernel, n, sky_count, taps, local),
        out_shape=jax.ShapeDtypeStruct((ROWS, COLS), f32),
        in_specs=[smem, anywhere, anywhere, anywhere],
        out_specs=vmem,
        scratch_shapes=[
            pltpu.VMEM((total + 2 * HALO, WIDE), bf),
            pltpu.VMEM((total + 2 * HALO, WIDE), f32),
            pltpu.VMEM((local, total, COLS), bf),
            pltpu.VMEM(column_mask.shape, jnp.int32),
            pltpu.VMEM((local, SUB, REACH), bf),
            pltpu.VMEM((REACH, local * SUB), bf),
            pltpu.VMEM((local, 512, 256), bf),
            pltpu.VMEM((CHUNK, WIDE), bf),
            pltpu.VMEM((CHUNK, COLS), bf),
            pltpu.VMEM((2, local * SUB, WIDE), bf),
            pltpu.VMEM((2, total, PAD), bf),
            pltpu.VMEM((2, total, PAD), bf),
            pltpu.VMEM((total, COLS), bf),
            pltpu.VMEM((total, COLS), bf),
            pltpu.VMEM((total, COLS), bf),
            pltpu.VMEM((total, COLS), bf),
            dma,
            dma((local,)),
            dma,
        ]
        + [dma((n, PARTS))] * 4
        + [dma((n,))] * 4
        + [dma((n * PARTS,))] * 8,
        compiler_params=pltpu.CompilerParams(
            collective_id=0, has_side_effects=True, vmem_limit_bytes=48 << 20
        ),
    )(scalars, column_mask, sky_scene, images)


def on_device(sky_scene, images, *rest):
    n = lax.axis_size("epoch")
    fits = (
        n == 4
        and sky_scene.shape == (ROWS, COLS)
        and images.shape[1:] == (n * ROWS, COLS)
        and images.shape[0] <= 2
    )
    plan = fused_plan if fits else strip_plan
    return plan(sky_scene, images, *rest)


def solution(mesh):
    return jax.shard_map(
        on_device,
        mesh=mesh,
        in_specs=(
            P(("field", "epoch"), "sky"),
            P(("field", "epoch"), None, "sky"),
            P("field", None),
            P("field", None),
            P("field", None),
            P("field"),
            P("field", "sky"),
            P("field", None, None),
        ),
        out_specs=P(("field", "epoch"), "sky"),
        check_vma=False,
    )
```

```python
import functools
import jax
import jax.numpy as jnp
from jax import lax
from jax.experimental import pallas as pl
from jax.experimental.pallas import tpu as pltpu
from jax.sharding import PartitionSpec as P

TILE = 512
HALO = 16
MESH = pl.DeviceIdType.MESH
ROWS = 512
COLS = 512
PAD = 128
WIDE = COLS + 2 * PAD
SUB = 128
REACH = SUB + 2 * HALO
CHUNK = 256
PARTS = ROWS // CHUNK


def extended(value, sides, width):
    for axis, dim in sides:
        peers, length = (lax.axis_size(axis), value.shape[dim])
        up = [(i, (i + 1) % peers) for i in range(peers - 1)]
        down = [(j, i) for i, j in up]
        last = lax.slice_in_dim(value, length - width, length, axis=dim)
        initial = lax.slice_in_dim(value, 0, width, axis=dim)
        before = lax.ppermute(last, axis, up)
        after = lax.ppermute(initial, axis, down)
        value = jnp.concatenate([before, value, after], axis=dim)
    return value


def band_tables(kernels, shifts, count_in, count_out):
    row_index = lax.broadcasted_iota(jnp.int32, (count_in, count_out), 0)
    col_index = lax.broadcasted_iota(jnp.int32, (count_in, count_out), 1)
    spread = kernels.shape[1]
    half_width = (spread - 1) // 2
    position = (
        (row_index - col_index)[None]
        - shifts[:, None, None]
        + half_width
        - (count_in - count_out) // 2
    )
    band_table = jnp.zeros((kernels.shape[0], count_in, count_out), jnp.float32)
    for each_tap in range(spread):
        band_table = band_table + jnp.where(
            position == each_tap, kernels[:, each_tap, None, None].astype(jnp.float32), 0.0
        )
    return band_table.astype(jnp.bfloat16)


def epoch_block(window, row_table, col_table, image_block, factor):
    lifted = jnp.einsum("ki,kc->ic", row_table, window, preferred_element_type=jnp.float32).astype(
        jnp.bfloat16
    )
    modeled = jnp.dot(lifted, col_table, preferred_element_type=jnp.float32)
    residual = (factor * (modeled - image_block.astype(jnp.float32))).astype(jnp.bfloat16)
    pulled = jnp.einsum(
        "ic,kc->ik", residual, col_table, preferred_element_type=jnp.float32
    ).astype(jnp.bfloat16)
    return jnp.dot(row_table, pulled, preferred_element_type=jnp.float32)


def strip_plan(sky_scene, images, psf_rows, psf_cols, offsets, epoch_weight, column_mask, coverage):
    slab_cells = extended(sky_scene, (("sky", 1),), HALO)
    strip_cells = lax.all_gather(slab_cells, "epoch", axis=0, tiled=True)
    strip_cells = jnp.pad(strip_cells, ((HALO, HALO), (0, 0)))
    full_rows = strip_cells.shape[0] - 2 * HALO
    strip_width = sky_scene.shape[1]
    local_count = images.shape[0]
    epoch_base = lax.axis_index("epoch") * local_count
    tile_column = lax.axis_index("sky") * strip_width // TILE

    def per_epoch(local_epoch, running):
        epoch_now = epoch_base + local_epoch
        row_table = band_tables(
            psf_rows[epoch_now][None], offsets[epoch_now, 0][None], TILE + 2 * HALO, TILE
        )[0]
        col_table = band_tables(
            psf_cols[epoch_now][None],
            offsets[epoch_now, 1][None],
            strip_width + 2 * HALO,
            strip_width,
        )[0]
        observed = lax.dynamic_index_in_dim(images, local_epoch, 0, keepdims=False)
        weight = epoch_weight[epoch_now]
        mask_row = column_mask[epoch_now].astype(jnp.float32)
        for row_block in range(full_rows // TILE):
            covered_flag = coverage[epoch_now, row_block, tile_column]
            window = strip_cells[row_block * TILE : row_block * TILE + TILE + 2 * HALO]
            image_block = observed[row_block * TILE : (row_block + 1) * TILE]
            factor = 2.0 * weight * covered_flag.astype(jnp.float32) * mask_row

            def covered():
                return epoch_block(window, row_table, col_table, image_block, factor)

            def skipped():
                return jnp.zeros((TILE + 2 * HALO, strip_width + 2 * HALO), jnp.float32)

            grad_term = lax.cond(covered_flag > 0, covered, skipped)
            running = running.at[row_block * TILE : row_block * TILE + TILE + 2 * HALO].add(
                grad_term
            )
        return running

    running = lax.fori_loop(
        0,
        local_count,
        per_epoch,
        jnp.zeros((full_rows + 2 * HALO, strip_width + 2 * HALO), jnp.float32),
    )
    trimmed = running[HALO : HALO + full_rows]
    packed = jnp.concatenate([trimmed[:, :HALO], trimmed[:, strip_width + HALO :]], axis=1)
    center_raw = trimmed[:, HALO : HALO + strip_width]
    received = extended(packed, (("sky", 1),), HALO)
    center_cells = center_raw.at[:, :HALO].add(received[:, :HALO])
    center_cells = center_cells.at[:, strip_width - HALO :].add(received[:, 3 * HALO :])
    return lax.psum_scatter(center_cells, "epoch", scatter_dimension=0, tiled=True)


def band(position, psf_ref, epoch, first, taps):
    table = jnp.zeros(position.shape, jnp.float32)
    for tap in range(taps):
        table = jnp.where(position == tap, psf_ref[epoch, first + tap], table)
    return table.astype(jnp.bfloat16)


def fused_kernel(
    n, sky_count, taps, local,
    psf_ref, offset_ref, factor_ref, mask_in, scene_ref, image_ref, out_ref,
    strip, acc, image_buf, mask_ref, row_tab, rowt_tab, col_tab, lift, res, pull,
    edge_out, edge_in, send_r, recv_r, send_l, recv_l,
    load_sem, image_sem, mask_sem,
    ag_r_send, ag_r_recv, ag_l_send, ag_l_recv,
    sky_r_send, sky_r_recv, sky_l_send, sky_l_recv,
    rs_r_send, rs_r_recv, rs_l_send, rs_l_recv,
    ed_r_send, ed_r_recv, ed_l_send, ed_l_recv,
):
    me = lax.axis_index("epoch")
    sky = lax.axis_index("sky")
    total = n * ROWS
    has_up, has_down = me > 0, me < n - 1
    has_left, has_right = sky > 0, sky < sky_count - 1
    base = me * local
    half = (taps - 1) // 2

    def rows_of(block, part=None):
        if part is None:
            return pl.ds(pl.multiple_of(HALO + block * ROWS, HALO), ROWS)
        return pl.ds(pl.multiple_of(HALO + block * ROWS + part * CHUNK, HALO), CHUNK)

    centre = pl.ds(PAD, COLS)
    load = pltpu.make_async_copy(scene_ref, strip.at[rows_of(me), centre], load_sem)
    load.start()
    mask_load = pltpu.make_async_copy(mask_in, mask_ref, mask_sem)
    mask_load.start()
    image_loads = [
        pltpu.make_async_copy(image_ref.at[e], image_buf.at[e], image_sem.at[e])
        for e in range(local)
    ]

    barrier = pltpu.get_barrier_semaphore()
    greetings = (
        (has_up, {"epoch": me - 1}),
        (has_down, {"epoch": me + 1}),
        (has_left, {"sky": sky - 1}),
        (has_right, {"sky": sky + 1}),
    )
    for there, where in greetings:
        @pl.when(there)
        def _():
            pl.semaphore_signal(barrier, inc=1, device_id=where, device_id_type=MESH)
    pl.semaphore_wait(barrier, sum(there.astype(jnp.int32) for there, where in greetings))

    def remote(src, dst, ssem, rsem, where):
        return pltpu.make_async_remote_copy(
            src_ref=src, dst_ref=dst, send_sem=ssem, recv_sem=rsem,
            device_id=where, device_id_type=MESH,
        )

    def gather_down(t, part):
        piece = strip.at[rows_of(me - t, part), centre]
        return remote(piece, piece, ag_r_send.at[t, part], ag_r_recv.at[t, part], {"epoch": me + 1})

    def gather_down_in(t, part):
        piece = strip.at[rows_of(me - 1 - t, part), centre]
        return remote(piece, piece, ag_r_send.at[t, part], ag_r_recv.at[t, part], {"epoch": me - 1})

    def gather_up(t, part):
        piece = strip.at[rows_of(me + t, part), centre]
        return remote(piece, piece, ag_l_send.at[t, part], ag_l_recv.at[t, part], {"epoch": me - 1})

    def gather_up_in(t, part):
        piece = strip.at[rows_of(me + 1 + t, part), centre]
        return remote(piece, piece, ag_l_send.at[t, part], ag_l_recv.at[t, part], {"epoch": me + 1})

    def sky_right(block):
        return remote(
            strip.at[rows_of(block), pl.ds(COLS, PAD)], strip.at[rows_of(block), pl.ds(0, PAD)],
            sky_r_send.at[block], sky_r_recv.at[block], {"sky": sky + 1},
        )

    def sky_right_in(block):
        return remote(
            strip.at[rows_of(block), pl.ds(COLS, PAD)], strip.at[rows_of(block), pl.ds(0, PAD)],
            sky_r_send.at[block], sky_r_recv.at[block], {"sky": sky - 1},
        )

    def sky_left(block):
        return remote(
            strip.at[rows_of(block), pl.ds(PAD, PAD)], strip.at[rows_of(block), pl.ds(PAD + COLS, PAD)],
            sky_l_send.at[block], sky_l_recv.at[block], {"sky": sky - 1},
        )

    def sky_left_in(block):
        return remote(
            strip.at[rows_of(block), pl.ds(PAD, PAD)], strip.at[rows_of(block), pl.ds(PAD + COLS, PAD)],
            sky_l_send.at[block], sky_l_recv.at[block], {"sky": sky + 1},
        )

    def send_edges(block):
        @pl.when(has_right)
        def _():
            sky_right(block).start()

        @pl.when(has_left)
        def _():
            sky_left(block).start()

    def wait_edges(block):
        @pl.when(has_left)
        def _():
            sky_right_in(block).wait_recv()

        @pl.when(has_right)
        def _():
            sky_left_in(block).wait_recv()

    load.wait()
    for part in range(PARTS):
        @pl.when(has_down)
        def _():
            gather_down(0, part).start()

        @pl.when(has_up)
        def _():
            gather_up(0, part).start()
    send_edges(me)
    for copy in image_loads:
        copy.start()

    strip[pl.ds(0, HALO), :] = jnp.zeros((HALO, WIDE), jnp.bfloat16)
    strip[pl.ds(HALO + total, HALO), :] = jnp.zeros((HALO, WIDE), jnp.bfloat16)

    @pl.when(sky == 0)
    def _():
        strip[pl.ds(HALO, total), pl.ds(0, PAD)] = jnp.zeros((total, PAD), jnp.bfloat16)

    @pl.when(sky == sky_count - 1)
    def _():
        strip[pl.ds(HALO, total), pl.ds(PAD + COLS, PAD)] = jnp.zeros((total, PAD), jnp.bfloat16)

    def clear(i, carry):
        acc[pl.ds(pl.multiple_of(i * 32, 32), 32), :] = jnp.zeros((32, WIDE), jnp.float32)
        return carry

    lax.fori_loop(0, (total + 2 * HALO) // 32, clear, 0)

    for e in range(local):
        shift_r = offset_ref[base + e, 0]
        shift_c = offset_ref[base + e, 1]
        out_i = lax.broadcasted_iota(jnp.int32, (SUB, REACH), 0)
        in_i = lax.broadcasted_iota(jnp.int32, (SUB, REACH), 1)
        row_tab[e] = band(in_i - out_i - HALO - shift_r + half, psf_ref, base + e, 0, taps)
        in_t = lax.broadcasted_iota(jnp.int32, (REACH, SUB), 0)
        out_t = lax.broadcasted_iota(jnp.int32, (REACH, SUB), 1)
        rowt_tab[:, e * SUB : (e + 1) * SUB] = band(
            in_t - out_t - HALO - shift_r + half, psf_ref, base + e, 0, taps
        )

        def fill(i, carry):
            k = lax.broadcasted_iota(jnp.int32, (64, 256), 0) + i * 64
            j = lax.broadcasted_iota(jnp.int32, (64, 256), 1)
            col_tab[e, pl.ds(pl.multiple_of(i * 64, 64), 64), :] = band(
                k - j - PAD - shift_c + half, psf_ref, base + e, taps, taps
            )
            return carry

        lax.fori_loop(0, 8, fill, 0)

    def compute(q, carry):
        r0 = pl.multiple_of(q * CHUNK, CHUNK)
        for e in range(local):
            for u in range(2):
                window = strip[pl.ds(pl.multiple_of(r0 + u * SUB, SUB), REACH), :]
                lift[u * SUB : (u + 1) * SUB, :] = jnp.dot(
                    row_tab[e], window, preferred_element_type=jnp.float32
                ).astype(jnp.bfloat16)
            factor = factor_ref[base + e, q // PARTS] * mask_ref[pl.ds(base + e, 1), :].astype(
                jnp.float32
            )
            for h in range(2):
                cols = slice(h * 256, (h + 1) * 256)
                modeled = jnp.dot(
                    lift[:, h * 256 : h * 256 + 512], col_tab[e], preferred_element_type=jnp.float32
                )
                seen = image_buf[e, pl.ds(r0, CHUNK), cols].astype(jnp.float32)
                res[:, cols] = (factor[:, cols] * (modeled - seen)).astype(jnp.bfloat16)

            def back(h, side):
                return lax.dot_general(
                    res[:, h * 256 : (h + 1) * 256],
                    col_tab[e, side * 256 : (side + 1) * 256, :],
                    (((1,), (1,)), ((), ())),
                    preferred_element_type=jnp.float32,
                )

            pulls = (back(0, 0), back(0, 1) + back(1, 0), back(1, 1))
            for third, value in enumerate(pulls):
                narrow = value.astype(jnp.bfloat16)
                for u in range(2):
                    pull[u, e * SUB : (e + 1) * SUB, third * 256 : (third + 1) * 256] = narrow[
                        u * SUB : (u + 1) * SUB
                    ]
        for u in range(2):
            where = pl.ds(pl.multiple_of(r0 + u * SUB, SUB), REACH)
            acc[where, :] += jnp.dot(rowt_tab[...], pull[u], preferred_element_type=jnp.float32)
        return carry

    mask_load.wait()
    for copy in image_loads:
        copy.wait()
    wait_edges(me)

    upper = me < n // 2
    near_low = jnp.where(upper, 0, n // 2)

    def ready(t):
        low = jnp.maximum(me - t, 0)
        high = jnp.minimum(me + t, n - 1)
        first = jnp.where(low == 0, 0, low + 1)
        stop = jnp.where(high == n - 1, n, high)
        return jnp.maximum(first, near_low), jnp.minimum(stop, near_low + n // 2)

    for t in range(n - 1):
        for part in range(PARTS):
            @pl.when(me - 1 - t >= 0)
            def _():
                gather_down_in(t, part).wait_recv()
                if t + 1 < n - 1:
                    @pl.when(has_down)
                    def _():
                        gather_down(t + 1, part).start()

            @pl.when(me + 1 + t <= n - 1)
            def _():
                gather_up_in(t, part).wait_recv()
                if t + 1 < n - 1:
                    @pl.when(has_up)
                    def _():
                        gather_up(t + 1, part).start()

        @pl.when(me - 1 - t >= 0)
        def _():
            send_edges(me - 1 - t)

        @pl.when(me + 1 + t <= n - 1)
        def _():
            send_edges(me + 1 + t)

        @pl.when(me - 1 - t >= 0)
        def _():
            wait_edges(me - 1 - t)

        @pl.when(me + 1 + t <= n - 1)
        def _():
            wait_edges(me + 1 + t)

        first, stop = ready(t + 1)
        if t == 0:
            lax.fori_loop(first * PARTS, stop * PARTS, compute, 0)
        elif t == 1:
            @pl.when((me == 0) | (me == n - 1))
            def _():
                block = jnp.where(upper, 1, n - 2)
                lax.fori_loop(block * PARTS, (block + 1) * PARTS, compute, 0)

    pieces = n * PARTS
    half_pieces = pieces // 2

    def far(i):
        return jnp.where(upper, pieces - 1 - i, i)

    def near(j):
        return jnp.where(upper, j, pieces - 1 - j)

    def flat(q):
        return pl.ds(pl.multiple_of(q * CHUNK, CHUNK), CHUNK)

    def mine(q):
        return pl.ds(pl.multiple_of(HALO + q * CHUNK, HALO), CHUNK)

    def grad_right(q, where):
        return remote(edge_out.at[1, flat(q)], edge_in.at[0, flat(q)], ed_r_send.at[q], ed_r_recv.at[q], where)

    def grad_left(q, where):
        return remote(edge_out.at[0, flat(q)], edge_in.at[1, flat(q)], ed_l_send.at[q], ed_l_recv.at[q], where)

    def share(q):
        @pl.when(has_right)
        def _():
            edge_out[1, flat(q), :] = acc[mine(q), PAD + COLS : WIDE].astype(jnp.bfloat16)
            grad_right(q, {"sky": sky + 1}).start()

        @pl.when(has_left)
        def _():
            edge_out[0, flat(q), :] = acc[mine(q), 0:PAD].astype(jnp.bfloat16)
            grad_left(q, {"sky": sky - 1}).start()

    def merge(q):
        @pl.when(has_left)
        def _():
            grad_right(q, {"sky": sky - 1}).wait_recv()
            acc[mine(q), PAD : 2 * PAD] += edge_in[0, flat(q), :].astype(jnp.float32)

        @pl.when(has_right)
        def _():
            grad_left(q, {"sky": sky + 1}).wait_recv()
            acc[mine(q), COLS : COLS + PAD] += edge_in[1, flat(q), :].astype(jnp.float32)

    def reduce_down(q, where):
        return remote(send_r.at[flat(q)], recv_r.at[flat(q)], rs_r_send.at[q], rs_r_recv.at[q], where)

    def reduce_up(q, where):
        return remote(send_l.at[flat(q)], recv_l.at[flat(q)], rs_l_send.at[q], rs_l_recv.at[q], where)

    def pass_on(q, down):
        staged, arrived = (send_r, recv_r) if down else (send_l, recv_l)
        move = reduce_down if down else reduce_up
        fed = has_up if down else has_down
        out_to = {"epoch": me + 1} if down else {"epoch": me - 1}
        in_from = {"epoch": me - 1} if down else {"epoch": me + 1}

        @pl.when(fed)
        def _():
            move(q, in_from).wait_recv()
            staged[flat(q), :] = (
                acc[mine(q), PAD : PAD + COLS] + arrived[flat(q), :].astype(jnp.float32)
            ).astype(jnp.bfloat16)

        @pl.when(jnp.logical_not(fed))
        def _():
            staged[flat(q), :] = acc[mine(q), PAD : PAD + COLS].astype(jnp.bfloat16)

        move(q, out_to).start()

    def pass_far(i):
        merge(far(i))

        @pl.when(upper)
        def _():
            pass_on(far(i), True)

        @pl.when(jnp.logical_not(upper))
        def _():
            pass_on(far(i), False)

    inner = (me > 0) & (me < n - 1)

    def pass_near(j):
        merge(near(j))
        inward = upper != inner

        @pl.when(inward)
        def _():
            pass_on(near(j), True)

        @pl.when(jnp.logical_not(inward))
        def _():
            pass_on(near(j), False)

    for j in range(half_pieces - 1):
        share(near(j))
    for i in range(half_pieces):
        compute(far(i), 0)
        if i >= 1:
            share(far(i - 1))
        if i >= 2:
            pass_far(i - 2)
    share(far(half_pieces - 1))
    share(near(half_pieces - 1))
    for i in range(half_pieces - 2, PARTS):
        pass_far(i)

    @pl.when(inner)
    def _():
        for j in range(PARTS):
            pass_near(j)

    for i in range(max(PARTS, half_pieces - 2), half_pieces):
        pass_far(i)

    @pl.when(jnp.logical_not(inner))
    def _():
        for j in range(PARTS, half_pieces):
            pass_near(j)

    for part in range(PARTS):
        rows = pl.ds(part * CHUNK, CHUNK)
        q = me * PARTS + part
        merge(q)
        out_ref[rows, :] = acc[mine(q), PAD : PAD + COLS]

        @pl.when(has_up)
        def _():
            reduce_down(q, {"epoch": me - 1}).wait_recv()
            out_ref[rows, :] += recv_r[flat(q), :].astype(jnp.float32)

        @pl.when(has_down)
        def _():
            reduce_up(q, {"epoch": me + 1}).wait_recv()
            out_ref[rows, :] += recv_l[flat(q), :].astype(jnp.float32)

    for t in range(n - 1):
        for part in range(PARTS):
            @pl.when(has_down & (me - t >= 0))
            def _():
                gather_down(t, part).wait_send()

            @pl.when(has_up & (me + t <= n - 1))
            def _():
                gather_up(t, part).wait_send()
    for q in range(pieces):
        @pl.when(me < q // PARTS)
        def _():
            reduce_down(q, {"epoch": me + 1}).wait_send()

        @pl.when(me > q // PARTS)
        def _():
            reduce_up(q, {"epoch": me - 1}).wait_send()

        @pl.when(has_right)
        def _():
            grad_right(q, {"sky": sky + 1}).wait_send()

        @pl.when(has_left)
        def _():
            grad_left(q, {"sky": sky - 1}).wait_send()
    for block in range(n):
        @pl.when(has_right)
        def _():
            sky_right(block).wait_send()

        @pl.when(has_left)
        def _():
            sky_left(block).wait_send()


def fused_plan(sky_scene, images, psf_rows, psf_cols, offsets, epoch_weight, column_mask, coverage):
    n, sky_count = lax.axis_size("epoch"), lax.axis_size("sky")
    local, total = images.shape[0], images.shape[1]
    taps = psf_rows.shape[1]
    psf = jnp.concatenate([psf_rows, psf_cols], axis=1).astype(jnp.float32)
    tile_column = lax.axis_index("sky") * COLS // TILE
    tiles = lax.dynamic_index_in_dim(coverage, tile_column, 2, keepdims=False)
    factor = 2.0 * epoch_weight[:, None] * tiles.astype(jnp.float32)
    bf, f32 = jnp.bfloat16, jnp.float32
    smem = pl.BlockSpec(memory_space=pltpu.SMEM)
    vmem = pl.BlockSpec(memory_space=pltpu.VMEM)
    anywhere = pl.BlockSpec(memory_space=pltpu.HBM)
    dma = pltpu.SemaphoreType.DMA
    return pl.pallas_call(
        functools.partial(fused_kernel, n, sky_count, taps, local),
        out_shape=jax.ShapeDtypeStruct((ROWS, COLS), f32),
        in_specs=[smem, smem, smem, anywhere, anywhere, anywhere],
        out_specs=vmem,
        scratch_shapes=[
            pltpu.VMEM((total + 2 * HALO, WIDE), bf),
            pltpu.VMEM((total + 2 * HALO, WIDE), f32),
            pltpu.VMEM((local, total, COLS), bf),
            pltpu.VMEM(column_mask.shape, jnp.int32),
            pltpu.VMEM((local, SUB, REACH), bf),
            pltpu.VMEM((REACH, local * SUB), bf),
            pltpu.VMEM((local, 512, 256), bf),
            pltpu.VMEM((CHUNK, WIDE), bf),
            pltpu.VMEM((CHUNK, COLS), bf),
            pltpu.VMEM((2, local * SUB, WIDE), bf),
            pltpu.VMEM((2, total, PAD), bf),
            pltpu.VMEM((2, total, PAD), bf),
            pltpu.VMEM((total, COLS), bf),
            pltpu.VMEM((total, COLS), bf),
            pltpu.VMEM((total, COLS), bf),
            pltpu.VMEM((total, COLS), bf),
            dma,
            dma((local,)),
            dma,
        ]
        + [dma((n, PARTS))] * 4
        + [dma((n,))] * 4
        + [dma((n * PARTS,))] * 8,
        compiler_params=pltpu.CompilerParams(
            collective_id=0, has_side_effects=True, vmem_limit_bytes=48 << 20
        ),
    )(psf, offsets, factor, column_mask, sky_scene, images)


def on_device(sky_scene, images, *rest):
    n = lax.axis_size("epoch")
    fits = (
        n == 4
        and sky_scene.shape == (ROWS, COLS)
        and images.shape[1:] == (n * ROWS, COLS)
        and images.shape[0] <= 2
    )
    plan = fused_plan if fits else strip_plan
    return plan(sky_scene, images, *rest)


def solution(mesh):
    return jax.shard_map(
        on_device,
        mesh=mesh,
        in_specs=(
            P(("field", "epoch"), "sky"),
            P(("field", "epoch"), None, "sky"),
            P("field", None),
            P("field", None),
            P("field", None),
            P("field"),
            P("field", "sky"),
            P("field", None, None),
        ),
        out_specs=P(("field", "epoch"), "sky"),
        check_vma=False,
    )
```
